128 devices in a mesh: seq: 16 (over x, z), exp: 8 (over y, core).
Axes of the slice: x: 4, y: 4, z: 4, core: 2. Of those that a mesh axis runs over, the one named last changes fastest.
Arguments:
- tokens: bfloat16 [16384, 1536], P(('seq', 'exp')), may hold values from -6 to 6
- in_gain: float32 [1536], replicated, may hold values from 0.5 to 1.5
- in_z: bfloat16 [1536, 3072], P(None, 'exp'), may hold values from -0.15625 to 0.15625
- in_x: bfloat16 [1536, 3072], P(None, 'exp'), may hold values from -0.15625 to 0.15625
- in_bc: bfloat16 [1536, 256], replicated, may hold values from -0.15625 to 0.15625
- in_dt: bfloat16 [1536, 48], P(None, 'exp'), may hold values from -0.0390625 to 0.0390625
- conv_x: float32 [4, 3072], P(None, 'exp'), may hold values from -3 to 3
- conv_bc: float32 [4, 256], replicated, may hold values from -3 to 3
- dt_bias: float32 [48], P('exp'), may hold values from -7 to -2
- a_log: float32 [48], P('exp'), may hold values from -1 to 2.5
- d_skip: float32 [48], P('exp'), may hold values from 0.5 to 1.5
- norm_gain: float32 [3072], P('exp'), may hold values from 0.5 to 1.5
- out_w: bfloat16 [3072, 1536], P('exp'), may hold values from -0.109375 to 0.109375
- post_gain: float32 [1536], replicated, may hold values from 0.5 to 1.5
- sh_gate: bfloat16 [1536, 1024], P(None, 'exp'), may hold values from -0.15625 to 0.15625
- sh_up: bfloat16 [1536, 1024], P(None, 'exp'), may hold values from -0.15625 to 0.15625
- sh_down: bfloat16 [1024, 1536], P('exp'), may hold values from -0.1875 to 0.1875
- ex_gate: bfloat16 [64, 1536, 512], P('seq'), may hold values from -0.15625 to 0.15625
- ex_up: bfloat16 [64, 1536, 512], P('seq'), may hold values from -0.15625 to 0.15625
- ex_down: bfloat16 [64, 512, 1536], P('seq'), may hold values from -0.25 to 0.25
- routes: int32 [16384, 6], P(('seq', 'exp')), may hold values from 0 to 63, all different within a row; in each aligned block of 128 rows (0 to 127, 128 to 255, ...) at most 16 rows name the same one
- gates: float32 [16384, 6], P(('seq', 'exp')), may hold values from 0.1 to 1
- lengths: int32 [16], replicated, may hold values from 1 to 4096, 16384 in all
- cache_slot: int32 [16], replicated, may hold values from 0 to 15, each once
Outputs:
- layer_out: bfloat16 [16384, 1536], P(('seq', 'exp'))
- state_cache: float32 [16, 48, 64, 128], P('seq', 'exp')
The draws below stay inside these ranges and needn't reach their ends.
Inputs may be any that keep to these rules, and one draw needn't show every extreme that they name: `routes`: in the rows of one device (aligned blocks of 128 rows) no expert is named by more than 16 rows, a bound that some block reaches; each row names 6 different experts. The lengths sum to 16384; the largest is exactly 4096. `cache_slot`: every slot is named once.
All inputs are finite; a program needn't handle non-finite values.
Results may differ from the reference program's by a relative error of at most 0.019.
Values may be sent and summed in bfloat16 or wider, within the bound.
No kernel may reach another device: no remote copies, remote signals or barrier semaphores. Data moves between devices by JAX's collectives and lax.ppermute only.
A program may use at most 128 MiB of HBM per device.

```python
import math
import jax
import jax.numpy as jnp
import numpy as np
from jax import lax

D = 1536
HEADS = 48
HDIM = 64
DSTATE = 128
CONV = 4
FFE = 512
FFS = 1024
TOP = 6
BLOCK = 512
TOK_DEV = 128
EXPERTS = 64
TOKENS = 16384
NREQ = 16
LONGEST = 4096
CAP = 16
DI = 3072
N_SEQ = 16
N_EXP = 8


def block_levels(rng, extent, split, low, high):
    loudness = 1.0
    for position, blocks in split:
        draws = jax.random.uniform(jax.random.fold_in(jax.random.fold_in(rng, 6), position), (blocks,), jnp.float32, low / len(split), high / len(split))
        loudness = loudness * jnp.repeat(jnp.exp(draws), extent[position] // blocks).reshape((-1,) + (1,) * (len(extent) - 1 - position))
    return loudness


def profile(amount, total, limit, lean):
    portions = [(1 << 20) // math.isqrt(standing ** lean) + 1 for standing in range(2, amount + 1)]
    surplus, given = total - limit - (amount - 1), [1] * (amount - 1)
    while surplus > 0:
        free = [i for i in range(amount - 1) if given[i] < limit]
        mass, remaining = sum([portions[i] for i in free]), surplus
        for i in free:
            addition = min(limit - given[i], max(1, remaining * portions[i] // mass), surplus)
            given[i] = given[i] + addition
            surplus = surplus - addition
    return np.array([limit] + given)


def ragged(key, count, total, most, lean):
    if count == 2:
        one = jax.random.randint(key, (), max(1, total - most), min(most, total - 1) + 1)
        return jnp.stack([one, total - one])
    sizes = jnp.asarray(profile(count, total, most, lean), jnp.int32)
    twos = (count - 1) // 2
    donor, taker = sizes[1:1 + 2 * twos:2], sizes[2:2 + 2 * twos:2]
    room = jnp.minimum(donor - 1, most - taker)
    moved = jax.random.randint(jax.random.fold_in(key, 1), (twos,), 0, 1 << 20) % (room + 1)
    sizes = sizes.at[1:1 + 2 * twos:2].set(donor - moved).at[2:2 + 2 * twos:2].set(taker + moved)
    return sizes[jax.random.permutation(jax.random.fold_in(key, 2), count)]


def deal_out(key, own, number, rows, amount, top, bound, slope):
    order = jax.random.permutation(key, amount)
    packed, ordinary = shares(amount, rows * top, bound, slope, True), shares(amount, rows * top, bound, slope, False)
    places = jnp.arange(amount)

    def named(sizes, rotation):
        used = int((sizes > 0).sum())
        fixed = max(1, used // 4)
        moved = fixed + (places - fixed + rotation * (used - fixed)) % max(1, amount - fixed)
        return jnp.zeros((amount,), jnp.int32).at[order[jnp.where(places < fixed, places, moved)]].set(jnp.asarray(sizes, jnp.int32))

    sizes = jnp.where(number % 4 == 0, named(packed, number // 4), named(ordinary, number - number // 4 - 1))
    mixed = jax.random.permutation(jax.random.fold_in(own, 3), amount)
    donor, receiver = mixed[0:amount // 2 * 2:2], mixed[1:amount // 2 * 2:2]
    margin = jnp.minimum(sizes[donor] - 1, bound - sizes[receiver]) // 2
    margin = jnp.where((donor == order[0]) | (receiver == order[0]) | (sizes[receiver] == 0), 0, jnp.maximum(margin, 0))
    moved = jax.random.randint(jax.random.fold_in(own, 4), (amount // 2,), 0, 1 << 20) % (margin + 1)
    sizes = sizes.at[donor].add(-moved).at[receiver].add(moved)
    labels = jnp.searchsorted(jnp.cumsum(sizes), jnp.arange(rows * top), side="right").astype(jnp.int32)
    listing = labels.reshape(top, rows).T
    listing = listing[jax.random.permutation(jax.random.fold_in(own, 1), rows)]
    rotation = jax.random.randint(jax.random.fold_in(own, 2), (rows, 1), 0, top)
    return jnp.take_along_axis(listing, (jnp.arange(top)[None, :] + rotation) % top, axis=1)


def shares(count, total, bound, lean, full):
    weights = [(1 << 20) // math.isqrt(grade ** lean) + 1 for grade in range(1, count + 1)]
    largest = bound if full else min(bound, max(-(-total // count), total * weights[0] // sum(weights)))
    least = 1 if total - largest >= count - 1 else 0
    holding, surplus = [largest] + [least] * (count - 1), total - largest - least * (count - 1)
    while surplus > 0:
        candidates = [i for i in range(1, count) if holding[i] < largest] or [i for i in range(1, count) if holding[i] < bound]
        whole, budget = sum([weights[i] for i in candidates]), surplus
        for i in candidates:
            addition = min(bound - holding[i], max(1, budget * weights[i] // whole), surplus)
            holding[i] = holding[i] + addition
            surplus = surplus - addition
    return np.array(holding)


def normal_values(key, shape, deviation, most, shards=(), kind=jnp.bfloat16):
    level = block_levels(key, shape, shards, -0.22, 0.18) if shards else 1.0
    values = jax.random.normal(key, shape, jnp.float32) * deviation * level
    return jnp.minimum(jnp.maximum(values, -most), most).astype(kind)


def setup_inputs(seed: int = 0) -> dict:
    splits = jax.random.split(jax.random.key(seed), 25)
    tokens = normal_values(splits[0], (TOKENS, D), 1.0, 6.0, ((0, 128),))
    in_gain = jnp.clip(1.0 + 0.1 * jax.random.normal(splits[1], (D,), jnp.float32), 0.5, 1.5)
    in_z = normal_values(splits[2], (D, DI), D ** -0.5, 0.15625, ((1, 8),))
    in_x = normal_values(splits[3], (D, DI), D ** -0.5, 0.15625, ((1, 8),))
    in_bc = normal_values(splits[4], (D, 2 * DSTATE), D ** -0.5, 0.15625)
    in_dt = normal_values(splits[5], (D, HEADS), (16 * D) ** -0.5, 0.0390625, ((1, 8),))
    conv_x = normal_values(splits[6], (CONV, DI), 0.5, 3.0, ((1, 8),), jnp.float32)
    conv_bc = normal_values(splits[7], (CONV, 2 * DSTATE), 0.5, 3.0, (), jnp.float32)
    dt_bias = jnp.clip(-7.0 + 5.0 * jax.random.uniform(splits[8], (HEADS,), jnp.float32) ** block_levels(splits[8], (HEADS,), ((0, 8),), -0.2, 0.2), -7.0, -2.0)
    a_log = jnp.clip(-1.0 + 3.5 * jax.random.uniform(splits[9], (HEADS,), jnp.float32) ** block_levels(splits[9], (HEADS,), ((0, 8),), -0.2, 0.2), -1.0, 2.5)
    d_skip = jnp.clip(0.5 + 1.0 * jax.random.uniform(splits[10], (HEADS,), jnp.float32) ** block_levels(splits[10], (HEADS,), ((0, 8),), -0.2, 0.2), 0.5, 1.5)
    norm_gain = jnp.clip(1.0 + 0.1 * jax.random.normal(splits[11], (DI,), jnp.float32), 0.5, 1.5)
    out_w = normal_values(splits[12], (DI, D), DI ** -0.5, 0.109375, ((0, 8),))
    post_gain = jnp.clip(1.0 + 0.1 * jax.random.normal(splits[13], (D,), jnp.float32), 0.5, 1.5)
    sh_gate = normal_values(splits[14], (D, FFS), D ** -0.5, 0.15625, ((1, 8),))
    sh_up = normal_values(splits[15], (D, FFS), D ** -0.5, 0.15625, ((1, 8),))
    sh_down = normal_values(splits[16], (FFS, D), FFS ** -0.5, 0.1875, ((0, 8),))
    ex_gate = normal_values(splits[17], (EXPERTS, D, FFE), D ** -0.5, 0.15625, ((0, 16),))
    ex_up = normal_values(splits[18], (EXPERTS, D, FFE), D ** -0.5, 0.15625, ((0, 16),))
    ex_down = normal_values(splits[19], (EXPERTS, FFE, D), FFE ** -0.5, 0.25, ((0, 16),))
    routes_keys = jax.random.split(jax.random.fold_in(splits[20], 1), TOKENS // TOK_DEV)
    routes_turns = jax.random.permutation(jax.random.fold_in(splits[20], 3), TOKENS // TOK_DEV)
    routes = jax.vmap(lambda own, number: deal_out(jax.random.fold_in(splits[20], 2), own, number, TOK_DEV, EXPERTS, TOP, CAP, 1))(routes_keys, routes_turns).reshape((TOKENS, TOP))
    gates = jnp.clip(0.1 + 0.9 * jax.random.uniform(splits[21], (TOKENS, TOP), jnp.float32) ** block_levels(splits[21], (TOKENS, TOP), ((0, 128),), -0.2, 0.2), 0.1, 1.0)
    lengths = ragged(splits[22], NREQ, TOKENS, LONGEST, 2).astype(jnp.int32)
    cache_slot = jax.random.permutation(splits[23], NREQ).astype(jnp.int32)
    return dict(tokens=tokens, in_gain=in_gain, in_z=in_z, in_x=in_x, in_bc=in_bc, in_dt=in_dt, conv_x=conv_x, conv_bc=conv_bc, dt_bias=dt_bias, a_log=a_log, d_skip=d_skip, norm_gain=norm_gain, out_w=out_w, post_gain=post_gain, sh_gate=sh_gate, sh_up=sh_up, sh_down=sh_down, ex_gate=ex_gate, ex_up=ex_up, ex_down=ex_down, routes=routes, gates=gates, lengths=lengths, cache_slot=cache_slot)


epsilon = 1e-05
highest = lax.Precision.HIGHEST

def rms_rows(values, gain):
    meansq = lax.optimization_barrier(jnp.mean(values * values, axis=-1, keepdims=True))
    return values * lax.rsqrt(meansq + epsilon) * gain

def segment_of(positions, req_ends):
    return lax.optimization_barrier(jnp.sum((positions[:, None] >= req_ends[None, :]).astype(jnp.int32), axis=1)).astype(jnp.int32)

def causal_conv(inputs, weight, segment):
    total = inputs.shape[0]
    summed = jnp.zeros(inputs.shape, jnp.float32)
    for tap in range(CONV):
        lag = CONV - 1 - tap
        shifted = jnp.pad(inputs.astype(jnp.float32), ((lag, 0), (0, 0)))[:total]
        earlier = jnp.pad(segment, (lag, 0), constant_values=-1)[:total]
        kept = (earlier == segment)[:, None]
        summed = summed + jnp.where(kept, weight[tap] * shifted, 0.0)
    return jax.nn.silu(summed).astype(jnp.bfloat16)

def block_step(state, block):
    drive_x, b_rows, c_rows, log_decay, step_size, segment, before_seg = block
    length = segment.shape[0]
    cumulative = jnp.cumsum(log_decay, axis=0)
    order = jnp.arange(length, dtype=jnp.int32)
    same = (segment[:, None] == segment[None, :]) & (order[:, None] >= order[None, :])
    log_gap = cumulative[:, None, :] - cumulative[None, :, :]
    decay = jnp.where(same[:, :, None], jnp.exp(jnp.where(same[:, :, None], log_gap, 0.0)), 0.0)
    scores = jnp.dot(c_rows, b_rows.T, preferred_element_type=jnp.float32)
    drive = drive_x.astype(jnp.float32) * step_size[:, :, None]
    weights = scores[:, :, None] * decay
    outputs = jnp.einsum('tsh,shp->thp', weights, drive, precision=highest)
    c_float = c_rows.astype(jnp.float32)
    b_float = b_rows.astype(jnp.float32)
    entry = jnp.where((segment == before_seg)[:, None], jnp.exp(cumulative), 0.0)
    outputs = outputs + entry[:, :, None] * jnp.einsum('tn,hpn->thp', c_float, state, precision=highest)
    last_seg = segment[length - 1]
    tail = jnp.where((segment == last_seg)[:, None], jnp.exp(cumulative[length - 1][None, :] - cumulative), 0.0)
    persist = jnp.where(last_seg == before_seg, jnp.exp(cumulative[length - 1]), 0.0)
    new_state = persist[:, None, None] * state + jnp.einsum('sh,shp,sn->hpn', tail, drive, b_float, precision=highest)
    return (new_state, outputs)

def reference(tokens, in_gain, in_z, in_x, in_bc, in_dt, conv_x, conv_bc, dt_bias, a_log, d_skip, norm_gain, out_w, post_gain, sh_gate, sh_up, sh_down, ex_gate, ex_up, ex_down, routes, gates, lengths, cache_slot):
    total = tokens.shape[0]
    normed_in = rms_rows(tokens.astype(jnp.float32), in_gain).astype(jnp.bfloat16)
    gate_raw = jnp.dot(normed_in, in_z, preferred_element_type=jnp.float32).astype(jnp.bfloat16)
    conv_in_x = jnp.dot(normed_in, in_x, preferred_element_type=jnp.float32).astype(jnp.bfloat16)
    conv_in_bc = jnp.dot(normed_in, in_bc, preferred_element_type=jnp.float32).astype(jnp.bfloat16)
    dt_raw = jnp.dot(normed_in, in_dt, preferred_element_type=jnp.float32).astype(jnp.bfloat16)
    req_ends = jnp.cumsum(lengths).astype(jnp.int32)
    positions = jnp.arange(total, dtype=jnp.int32)
    segment = segment_of(positions, req_ends)
    conv_x_out = causal_conv(conv_in_x, conv_x, segment)
    conv_bc_out = causal_conv(conv_in_bc, conv_bc, segment)
    b_all = conv_bc_out[:, :DSTATE]
    c_all = conv_bc_out[:, DSTATE:]
    step_size = jax.nn.softplus(dt_raw.astype(jnp.float32) + dt_bias)
    log_decay = -step_size * jnp.exp(a_log)
    heads_x = conv_x_out.reshape(total, HEADS, HDIM)
    before_all = jnp.concatenate([jnp.full((1,), -1, jnp.int32), segment[:-1]])
    count = total // BLOCK

    def blocked(values):
        return values.reshape((count, BLOCK) + values.shape[1:])
    blocks = (blocked(heads_x), blocked(b_all), blocked(c_all), blocked(log_decay), blocked(step_size), blocked(segment), blocked(before_all)[:, 0])
    start_state = jnp.zeros((HEADS, HDIM, DSTATE), jnp.float32)
    final_state, outputs = lax.scan(block_step, start_state, blocks)
    mixed_y = outputs.reshape(total, HEADS, HDIM) + d_skip[None, :, None] * heads_x.astype(jnp.float32)
    gated = mixed_y.reshape(total, DI) * jax.nn.silu(gate_raw.astype(jnp.float32))
    meansq = lax.optimization_barrier(jnp.sum(gated * gated, axis=1)) / DI
    scaled = (gated * lax.rsqrt(meansq + epsilon)[:, None] * norm_gain).astype(jnp.bfloat16)
    group_width = DI // N_EXP
    mixer_out = jnp.zeros((total, D), jnp.float32)
    for group_idx in range(N_EXP):
        lo_col = group_idx * group_width
        term = jnp.dot(scaled[:, lo_col:lo_col + group_width], out_w[lo_col:lo_col + group_width], preferred_element_type=jnp.float32)
        mixer_out = mixer_out + lax.optimization_barrier(term.astype(jnp.bfloat16)).astype(jnp.float32)
    residual = tokens.astype(jnp.float32) + mixer_out
    normed = rms_rows(residual, post_gain).astype(jnp.bfloat16)
    shared_hidden = (jax.nn.silu(jnp.dot(normed, sh_gate, preferred_element_type=jnp.float32)) * jnp.dot(normed, sh_up, preferred_element_type=jnp.float32)).astype(jnp.bfloat16)
    shared_width = FFS // N_EXP
    shared = jnp.zeros((total, D), jnp.float32)
    for group_idx in range(N_EXP):
        lo_col = group_idx * shared_width
        term = jnp.dot(shared_hidden[:, lo_col:lo_col + shared_width], sh_down[lo_col:lo_col + shared_width], preferred_element_type=jnp.float32)
        shared = shared + lax.optimization_barrier(term.astype(jnp.bfloat16)).astype(jnp.float32)
    flat_routes = routes.reshape(-1)
    flat_gates = gates.reshape(-1)
    most_rows = CAP * N_SEQ * N_EXP

    def expert_pass(routed, item):
        gate_e, up_e, down_e, expert_id = item
        chosen = flat_routes == expert_id
        found = jnp.nonzero(chosen, size=most_rows, fill_value=0)[0].astype(jnp.int32)
        valid = jnp.arange(most_rows, dtype=jnp.int32) < jnp.sum(chosen.astype(jnp.int32)).astype(jnp.int32)
        token_idx = found // TOP
        rows_in = normed[token_idx]
        hidden = (jax.nn.silu(jnp.dot(rows_in, gate_e, preferred_element_type=jnp.float32)) * jnp.dot(rows_in, up_e, preferred_element_type=jnp.float32)).astype(jnp.bfloat16)
        result = jnp.dot(hidden, down_e, preferred_element_type=jnp.float32).astype(jnp.bfloat16)
        weight_rows = jnp.where(valid, flat_gates[found], 0.0)
        routed = routed.at[token_idx].add(weight_rows[:, None] * result.astype(jnp.float32))
        return (routed, None)
    routed, _ = lax.scan(expert_pass, jnp.zeros((total, D), jnp.float32), (ex_gate, ex_up, ex_down, jnp.arange(ex_gate.shape[0], dtype=jnp.int32)))
    layer_out = (residual + shared + routed).astype(jnp.bfloat16)
    req_starts = (req_ends - lengths).astype(jnp.int32)
    pad_x = jnp.concatenate([heads_x.astype(jnp.float32) * step_size[:, :, None], jnp.zeros((LONGEST, HEADS, HDIM), jnp.float32)])
    pad_b = jnp.concatenate([b_all.astype(jnp.float32), jnp.zeros((LONGEST, DSTATE), jnp.float32)])
    pad_decay = jnp.concatenate([log_decay, jnp.zeros((LONGEST, HEADS), jnp.float32)])

    def request_state(req_idx):
        start = req_starts[req_idx]
        kept = jnp.arange(LONGEST, dtype=jnp.int32) < lengths[req_idx]
        drive = lax.dynamic_slice_in_dim(pad_x, start, LONGEST, 0)
        b_rows = lax.dynamic_slice_in_dim(pad_b, start, LONGEST, 0)
        decay_rows = jnp.where(kept[:, None], lax.dynamic_slice_in_dim(pad_decay, start, LONGEST, 0), 0.0)
        suffix = jnp.cumsum(decay_rows[::-1], axis=0)[::-1]
        after = jnp.concatenate([suffix[1:], jnp.zeros((1, HEADS), jnp.float32)])
        weights = jnp.where(kept[:, None], jnp.exp(after), 0.0)
        return jnp.einsum('sh,shp,sn->hpn', weights, drive, b_rows, precision=highest)
    states = lax.map(request_state, jnp.arange(NREQ, dtype=jnp.int32))
    state_cache = jnp.zeros((NREQ, HEADS, HDIM, DSTATE), jnp.float32).at[cache_slot].set(states)
    return (layer_out, state_cache)
```

```python
import functools

import jax
import jax.numpy as jnp
from jax import lax
from jax.experimental import pallas as pl
from jax.experimental.pallas import tpu as pltpu
from jax.sharding import PartitionSpec as P

EPS = 1e-05
HIGH = lax.Precision.HIGHEST
F32 = jnp.float32
BF16 = jnp.bfloat16
LANES = 128
ROWS = 128
CHUNK = 128
CAP = 16
HEADS = 6
HALF = 64
WIDE = 384
STATE = 128
DI = 3072
VM = pl.BlockSpec(memory_space=pltpu.VMEM)
SM = pl.BlockSpec(memory_space=pltpu.SMEM)
PLUS = [(i, (i + 2) % 8) for i in range(8)]
MINUS = [(i, (i + 6) % 8) for i in range(8)]
MATE = [(i, i ^ 1) for i in range(8)]


def silu(v):
    return v * (1.0 / (1.0 + jnp.exp(-v)))


def ahead(block, distance):
    return lax.ppermute(block, "seq", [(i, i + distance) for i in range(16 - distance)])


def over_exp(block, route):
    return lax.ppermute(block, "exp", route)


def spread(cols):
    rows = cols.shape[0]
    left = lax.broadcasted_iota(jnp.int32, (rows, LANES), 1) < HALF
    parts = []
    for pair in range(HEADS // 2):
        first = jnp.broadcast_to(cols[:, 2 * pair : 2 * pair + 1], (rows, LANES))
        second = jnp.broadcast_to(cols[:, 2 * pair + 1 : 2 * pair + 2], (rows, LANES))
        parts.append(jnp.where(left, first, second))
    return jnp.concatenate(parts, axis=1)


def gather_exp(own):
    half = own.shape[0] // 2
    up = over_exp(own, PLUS)
    down = over_exp(own, MINUS)
    mate = over_exp(own, MATE)
    far_a = over_exp(up[:half], PLUS)
    far_b = over_exp(down[half:], MINUS)
    up_mate = over_exp(up, MATE)
    down_mate = over_exp(down, MATE)
    far = jnp.concatenate([far_a, far_b])
    far_mate = over_exp(far, MATE)
    return (own, mate, up, up_mate, down, down_mate, far, far_mate)


def project_kernel(where_ref, b0, b1, b2, b3, b4, b5, b6, b7, gain, w_conv, w_dt, w_z, bias, conv_out, step_out, z_out, normed):
    chip = where_ref[0] // 2
    core = lax.rem(where_ref[0], 2)
    for slot, (pair, offset) in enumerate((((b0, b1), 0), ((b2, b3), 3), ((b4, b5), 1), ((b6, b7), 2))):
        for ref, place in ((pair[0], core), (pair[1], 1 - core)):
            vals = ref[...].astype(F32)
            meansq = jnp.mean(vals * vals, axis=-1, keepdims=True)
            start = pl.multiple_of(place * ROWS, ROWS)
            normed[pl.ds(start, ROWS), :] = (vals * lax.rsqrt(meansq + EPS) * gain[...]).astype(BF16)
        rows = normed[...]
        start = pl.multiple_of(lax.rem(chip + offset, 4) * (2 * ROWS), 2 * ROWS)
        conv_out[pl.ds(start, 2 * ROWS), :] = jnp.dot(rows, w_conv[...], preferred_element_type=F32).astype(BF16)
        raw = jnp.dot(rows, w_dt[...], preferred_element_type=F32).astype(BF16).astype(F32) + bias[...]
        step_out[pl.ds(start, 2 * ROWS), :] = jnp.maximum(raw, 0.0) + jnp.log1p(jnp.exp(-jnp.abs(raw)))
        gate = jnp.dot(rows, w_z[...], preferred_element_type=F32).astype(BF16).astype(F32)
        z_out[pl.ds(start, 2 * ROWS), :] = silu(gate)


def scan_kernel(meta, conv_in, edge, keep, seg_col, step_in, rate, w_conv, x_out, bc_out, cum_out, lead_out, state_out, send_out, state):
    state[...] = jnp.zeros_like(state)
    rows_i = lax.broadcasted_iota(jnp.int32, (CHUNK, CHUNK), 0)
    cols_i = lax.broadcasted_iota(jnp.int32, (CHUNK, CHUNK), 1)
    lower = (rows_i >= cols_i).astype(F32)
    before_dev = meta[0]

    def chunk(c, past):
        start = pl.multiple_of(c * CHUNK, CHUNK)
        prior_at = pl.multiple_of(jnp.maximum(start - 16, 0), 16)
        prior = jnp.where(c == 0, edge[...].astype(F32), conv_in[pl.ds(prior_at, 16), :].astype(F32))
        here = conv_in[pl.ds(start, CHUNK), :].astype(F32)
        joined = jnp.concatenate([prior, here], axis=0)
        kept = keep[pl.ds(start, CHUNK), :]
        total = here * w_conv[3:4, :]
        for lag in (1, 2, 3):
            moved = pltpu.roll(joined, lag, 0)[16:, :]
            total = total + (kept[:, lag : lag + 1] * moved) * w_conv[3 - lag : 4 - lag, :]
        mixed = silu(total).astype(BF16)
        x_out[pl.ds(start, CHUNK), :] = mixed[:, :WIDE]
        bc_out[pl.ds(start, CHUNK), :] = mixed[:, WIDE:]
        step = step_in[pl.ds(start, CHUNK), :]
        decay = -step * rate[...]
        cum = jnp.dot(lower, decay, precision=HIGH, preferred_element_type=F32)
        cum_out[pl.ds(start, CHUNK), :] = cum
        seg = seg_col[pl.ds(start, CHUNK), :]
        lead_out[pl.ds(start, CHUNK), :] = jnp.where(seg == before_dev, jnp.exp(past + cum), 0.0)
        last = cum[CHUNK - 1 : CHUNK, :]
        last_seg = meta[8 + 8 + c]
        tail = jnp.where(seg == last_seg, jnp.exp(last - cum), 0.0)
        drive = mixed[:, :WIDE].astype(F32) * spread(step * tail)
        fresh = lax.dot_general(
            mixed[:, WIDE : WIDE + STATE], drive.astype(BF16), (((0,), (0,)), ((), ())), preferred_element_type=F32
        )
        held = state[...]
        state_out[c] = held.astype(BF16)
        persist = jnp.where(last_seg == meta[8 + c], jnp.exp(last), 0.0)
        state[...] = spread(jnp.broadcast_to(persist, (8, LANES)))[:1, :] * held + fresh
        return past + last

    past = lax.fori_loop(0, 8, chunk, jnp.zeros((1, LANES), F32))
    send_out[:STATE, :] = state[...].astype(BF16)
    passed = jnp.where(meta[8 + 8 + 7] == before_dev, jnp.exp(past), 0.0)
    wide = spread(jnp.broadcast_to(passed, (16, LANES)))
    high = wide.astype(BF16)
    low = (wide - high.astype(F32)).astype(BF16)
    row = lax.broadcasted_iota(jnp.int32, (16, WIDE), 0)
    send_out[STATE:, :] = jnp.where(row == 0, high, low)


def local_kernel(meta, x_in, bc_in, cum_in, step_in, seg_col, seg_row, state_in, skip, y_out, ends_out):
    rows_i = lax.broadcasted_iota(jnp.int32, (CHUNK, CHUNK), 0)
    cols_i = lax.broadcasted_iota(jnp.int32, (CHUNK, CHUNK), 1)
    causal = rows_i >= cols_i
    left = lax.broadcasted_iota(jnp.int32, (CHUNK, LANES), 1) < HALF

    def chunk(c, carry):
        start = pl.multiple_of(c * CHUNK, CHUNK)
        x = x_in[pl.ds(start, CHUNK), :].astype(F32)
        bc = bc_in[pl.ds(start, CHUNK), :]
        b_rows, c_rows = bc[:, :STATE], bc[:, STATE:]
        cum = cum_in[pl.ds(start, CHUNK), :]
        cum_t = cum.T
        seg = seg_col[pl.ds(start, CHUNK), :]
        mask = causal & (seg == seg_row[pl.ds(c, 1), :])
        scores = lax.dot_general(c_rows, b_rows, (((1,), (1,)), ((), ())), preferred_element_type=F32)
        scores = jnp.where(mask, scores, 0.0)
        drive = x * spread(step_in[pl.ds(start, CHUNK), :])
        drive_b = drive.astype(BF16)
        held = state_in[c]
        before = meta[8 + c]
        entry = jnp.where(seg == before, jnp.exp(cum), 0.0)
        carried = jnp.dot(c_rows, held, preferred_element_type=F32)
        total = spread(entry) * carried + skip[...] * x
        parts = []
        for pair in range(HEADS // 2):
            block = drive_b[:, pair * LANES : (pair + 1) * LANES]
            zero = jnp.zeros_like(block)
            acc = None
            for side in (0, 1):
                head = 2 * pair + side
                gap = jnp.minimum(cum[:, head : head + 1] - cum_t[head : head + 1, :], 0.0)
                weights = (scores * jnp.exp(gap)).astype(BF16)
                value = jnp.where(left, block, zero) if side == 0 else jnp.where(left, zero, block)
                term = jnp.dot(weights, value, preferred_element_type=F32)
                acc = term if acc is None else acc + term
            parts.append(acc)
        y_out[pl.ds(start, CHUNK), :] = total + jnp.concatenate(parts, axis=1)
        held_f = held.astype(F32)

        def close(req, inner):
            at = meta[32 + req] - start

            @pl.when((at >= 0) & (at < CHUNK))
            def _():
                cum_end = cum_in[pl.ds(start + at, 1), :]
                weight = jnp.where(seg == req, jnp.exp(jnp.minimum(cum_end - cum, 0.0)), 0.0)
                fresh = lax.dot_general(
                    b_rows, (drive * spread(weight)).astype(BF16), (((0,), (0,)), ((), ())), preferred_element_type=F32
                )
                hold = jnp.where(req == before, jnp.exp(cum_end), 0.0)
                hold = spread(jnp.broadcast_to(hold, (8, LANES)))[:1, :]
                ends_out[meta[48 + req]] = (fresh + hold * held_f).astype(BF16)

            return inner

        lax.fori_loop(meta[24 + c], meta[8 + 8 + c] + 1, close, 0)
        return carry

    lax.fori_loop(0, 8, chunk, 0)


def out_kernel(where_ref, y_in, bc_in, lead_in, z_in, state_in, norm_gain, w_out, out, gated, squares, *, mate):
    chip = where_ref[0] // 2
    core = lax.rem(where_ref[0], 2)
    if mate:
        core = 1 - core
    for rel in range(4):
        start = pl.multiple_of((lax.rem(chip + rel, 4) * 2 + core) * ROWS, ROWS)
        c_rows = bc_in[pl.ds(start, ROWS), STATE:]
        carried = jnp.dot(c_rows, state_in[...], preferred_element_type=F32)
        y = y_in[pl.ds(start, ROWS), :] + spread(lead_in[pl.ds(start, ROWS), :]) * carried
        g = y * z_in[pl.ds(start, ROWS), :]
        out[rel, :, 1536:] = jnp.broadcast_to(jnp.sum(g * g, axis=1, keepdims=True), (ROWS, LANES)).astype(BF16)
        gated[rel * ROWS : (rel + 1) * ROWS, :] = (g * norm_gain[...]).astype(BF16)
    for rel in range(4):
        out[rel, :, :1536] = jnp.dot(
            gated[rel * ROWS : (rel + 1) * ROWS, :], w_out[...], preferred_element_type=F32
        ).astype(BF16)


def enter_kernel(h0, p_a, p_b, q_a, q_b, tokens, gain, spots, residual_out, normed_out, outgoing):
    first = h0[:HALF, :] + p_b[:HALF, :].astype(F32) + q_a[...].astype(F32)
    second = h0[HALF:, :] + p_a[HALF:, :].astype(F32) + q_b[...].astype(F32)
    both = jnp.concatenate([first, second], axis=0)
    scale = lax.rsqrt(both[:, 1536:1537] * (1.0 / DI) + EPS)
    residual = tokens[...].astype(F32) + both[:, :1536] * scale
    residual_out[...] = residual
    meansq = jnp.mean(residual * residual, axis=-1, keepdims=True)
    normed = (residual * lax.rsqrt(meansq + EPS) * gain[...]).astype(BF16)
    normed_out[...] = normed
    outgoing[...] = jnp.dot(spots[...], normed, preferred_element_type=F32).astype(BF16)


def expert_kernel(rows_ref, gate, up, down, out):
    rows = rows_ref[...].reshape(256, 1536)
    g = jnp.dot(rows, gate[...], preferred_element_type=F32)
    u = jnp.dot(rows, up[...], preferred_element_type=F32)
    hidden = (silu(g) * u).astype(BF16)
    out[...] = jnp.dot(hidden, down[...], preferred_element_type=F32).astype(BF16).reshape(16, CAP, 1536)


def shared_kernel(rows_ref, w0, w1, w2, w3, w4, w5, w6, w7, residual, out):
    rows = rows_ref[...]
    total = residual[...]
    for w in (w0, w1, w2, w3, w4, w5, w6, w7):
        both = lax.dot_general(rows, w[:256, :], (((1,), (1,)), ((), ())), preferred_element_type=F32)
        hidden = (silu(both[:, :128]) * both[:, 128:]).astype(BF16)
        total = total + jnp.dot(hidden, w[256:, :], preferred_element_type=F32)
    out[...] = total


def leave_kernel(returned, high, low, base, out):
    rows = returned[...]
    routed = jnp.dot(high[...], rows, preferred_element_type=F32) + jnp.dot(low[...], rows, preferred_element_type=F32)
    out[...] = (base[...] + routed).astype(BF16)


def shape(dims, dtype):
    return jax.ShapeDtypeStruct(dims, dtype)


def body(
    tokens,
    in_gain,
    in_z,
    in_x,
    in_bc,
    in_dt,
    conv_x,
    conv_bc,
    dt_bias,
    a_log,
    d_skip,
    norm_gain,
    out_w,
    post_gain,
    sh_gate,
    sh_up,
    sh_down,
    ex_gate,
    ex_up,
    ex_down,
    routes,
    gates,
    lengths,
    cache_slot,
):
    seq_idx = lax.axis_index("seq")
    exp_idx = lax.axis_index("exp")
    where_am_i = jnp.reshape(exp_idx, (1,)).astype(jnp.int32)
    width = tokens.shape[1]
    row_count = 8 * ROWS
    pad_heads = ((0, LANES - HEADS),)

    blocks = gather_exp(tokens)

    reqs = jnp.arange(16, dtype=jnp.int32)
    ends = jnp.sum(jnp.where(reqs[:, None] >= reqs[None, :], lengths[None, :], 0), axis=1)
    stream_start = (seq_idx * row_count).astype(jnp.int32)

    def seg_at(positions):
        found = jnp.sum((positions[..., None] >= ends).astype(jnp.int32), axis=-1)
        return jnp.where(positions >= 0, found, -1)

    local = jnp.arange(row_count, dtype=jnp.int32)
    segment = seg_at(stream_start + local)
    seg_col = segment[:, None]
    seg_row = segment.reshape(8, CHUNK)
    keep = jnp.stack(
        [(seg_at(stream_start + local - lag) == segment).astype(F32) for lag in range(4)], axis=1
    )
    bases = stream_start + CHUNK * jnp.arange(8, dtype=jnp.int32)
    before = seg_at(bases - 1)
    meta = jnp.concatenate(
        [before, before, seg_at(bases + CHUNK - 1), seg_at(bases), ends - 1 - stream_start, cache_slot]
    ).astype(jnp.int32)
    before_dev = before[0]

    picks = (routes[:, :, None] == jnp.arange(64, dtype=jnp.int32)).astype(F32)
    named = jnp.sum(picks, axis=1)
    weight = jnp.sum(picks * gates[:, :, None], axis=1)
    earlier = (jnp.arange(ROWS)[:, None] > jnp.arange(ROWS)[None, :]).astype(BF16)
    rank = jnp.dot(earlier, named.astype(BF16), preferred_element_type=F32)
    rank = jnp.where(named > 0, rank, -1.0)
    slots = jnp.arange(1024, dtype=jnp.int32)
    fan = (slots[None, :] // CAP == jnp.arange(64, dtype=jnp.int32)[:, None]).astype(BF16)
    rank_wide = jnp.dot(rank.astype(BF16), fan, preferred_element_type=F32)
    hit = rank_wide == (slots % CAP).astype(F32)[None, :]
    w_high = weight.astype(BF16)
    w_low = (weight - w_high.astype(F32)).astype(BF16)
    mix_high = jnp.where(hit, jnp.dot(w_high, fan, preferred_element_type=F32), 0.0).astype(BF16)
    mix_low = jnp.where(hit, jnp.dot(w_low, fan, preferred_element_type=F32), 0.0).astype(BF16)
    spots = hit.astype(BF16).T

    w_conv_in = jnp.concatenate([in_x, in_bc], axis=1)
    w_dt = jnp.pad(in_dt, ((0, 0),) + pad_heads)
    bias = jnp.pad(dt_bias, pad_heads)[None, :]
    rate = jnp.pad(jnp.exp(a_log), pad_heads)[None, :]
    taps = jnp.concatenate([conv_x, conv_bc], axis=1)
    skip = jnp.repeat(d_skip, HALF)[None, :]

    conv_in, step, z = pl.pallas_call(
        project_kernel,
        out_shape=(shape((row_count, 640), BF16), shape((row_count, LANES), F32), shape((row_count, WIDE), F32)),
        in_specs=[SM] + [VM] * 13,
        out_specs=(VM, VM, VM),
        scratch_shapes=[pltpu.VMEM((2 * ROWS, width), BF16)],
        name="project",
    )(where_am_i, *blocks, in_gain[None, :], w_conv_in, w_dt, in_z, bias)

    edge = ahead(conv_in[row_count - 16 :], 1)
    x_rows, bc_rows, cum, lead, states, sent = pl.pallas_call(
        scan_kernel,
        out_shape=(
            shape((row_count, WIDE), BF16),
            shape((row_count, 2 * STATE), BF16),
            shape((row_count, LANES), F32),
            shape((row_count, LANES), F32),
            shape((8, STATE, WIDE), BF16),
            shape((STATE + 16, WIDE), BF16),
        ),
        in_specs=[SM] + [VM] * 7,
        out_specs=(VM,) * 6,
        scratch_shapes=[pltpu.VMEM((STATE, WIDE), F32)],
        name="scan",
    )(meta, conv_in, edge, keep, seg_col, step, rate, taps)

    def split(message):
        factor = message[STATE : STATE + 1].astype(F32) + message[STATE + 1 : STATE + 2].astype(F32)
        return message[:STATE].astype(F32), factor

    def joined(state, factor):
        high = factor.astype(BF16)
        low = (factor - high.astype(F32)).astype(BF16)
        return jnp.concatenate([state.astype(BF16), high, low, jnp.zeros((14, WIDE), BF16)])

    got = ahead(sent, 1)
    y_local, ends_local = pl.pallas_call(
        local_kernel,
        out_shape=(shape((row_count, WIDE), F32), shape((16, STATE, WIDE), BF16)),
        in_specs=[SM] + [VM] * 8,
        out_specs=(VM, VM),
        name="local",
    )(meta, x_rows, bc_rows, cum, step, seg_col, seg_row, states, skip)
    own_state, own_factor = split(sent)
    got_state, got_factor = split(got)
    two = joined(own_state + own_factor * got_state, own_factor * got_factor)
    near_state, near_factor = split(ahead(two, 1))
    entering = near_state + near_factor * ahead(two[:STATE], 3).astype(F32)
    entering_b = entering.astype(BF16)

    open_req = jnp.maximum(before_dev, 0)
    open_end = meta[32 + open_req]
    holds = (before_dev >= 0) & (open_end >= 0) & (open_end < row_count)
    hold_row = lax.dynamic_slice_in_dim(lead, jnp.clip(open_end, 0, row_count - 1), 1, 0)
    hold_row = jnp.where(holds, jnp.repeat(hold_row[:, :HEADS], HALF, axis=1), 0.0)
    open_slot = cache_slot[open_req]
    open_value = lax.dynamic_index_in_dim(ends_local, open_slot, 0, False).astype(F32)
    open_value = jnp.where(holds, open_value + hold_row * entering, open_value).astype(BF16)
    ends_local = lax.dynamic_update_index_in_dim(ends_local, open_value, open_slot, 0)
    ends_all = lax.all_to_all(ends_local, "seq", split_axis=0, concat_axis=0, tiled=True)
    my_req = jnp.sum(jnp.where(cache_slot == seq_idx, reqs, 0))
    source = (ends[my_req] - 1) // row_count
    final = lax.dynamic_index_in_dim(ends_all, source, 0, False).astype(F32)
    state_cache = final.T.reshape(1, HEADS, HALF, STATE)

    def project_out(mate):
        return pl.pallas_call(
            functools.partial(out_kernel, mate=mate),
            out_shape=shape((4, ROWS, width + LANES), BF16),
            in_specs=[SM] + [VM] * 7,
            out_specs=VM,
            scratch_shapes=[pltpu.VMEM((4 * ROWS, WIDE), BF16), pltpu.VMEM((8, LANES), F32)],
            name="out_mate" if mate else "out_own",
        )(where_am_i, y_local, bc_rows, lead, z, entering_b, norm_gain[None, :], out_w)

    swapped = over_exp(project_out(True), MATE)
    summed = project_out(False).astype(F32) + swapped.astype(F32)
    h0, h1, h2, h3 = summed[0], summed[1], summed[2], summed[3]
    p_a = over_exp(jnp.concatenate([h2[:HALF], h1[HALF:]]).astype(BF16), PLUS)
    p_b = over_exp(jnp.concatenate([h3[:HALF], h2[HALF:]]).astype(BF16), MINUS)
    q_a = over_exp((h1[:HALF] + p_a[:HALF].astype(F32)).astype(BF16), PLUS)
    q_b = over_exp((h3[HALF:] + p_b[HALF:].astype(F32)).astype(BF16), MINUS)

    residual, normed, outgoing = pl.pallas_call(
        enter_kernel,
        out_shape=(shape((ROWS, width), F32), shape((ROWS, width), BF16), shape((1024, width), BF16)),
        in_specs=[VM] * 8,
        out_specs=(VM, VM, VM),
        name="enter",
    )(h0, p_a, p_b, q_a, q_b, tokens, post_gain[None, :], spots)

    received = lax.all_to_all(
        outgoing.reshape(16, 4, CAP, width), "seq", split_axis=0, concat_axis=0, tiled=True
    )
    packed = jnp.concatenate([sh_gate.T, sh_up.T, sh_down])
    packed, normed = lax.optimization_barrier((packed, normed))
    groups = gather_exp(packed)
    base = pl.pallas_call(
        shared_kernel,
        out_shape=shape((ROWS, width), F32),
        in_specs=[VM] * 10,
        out_specs=VM,
        name="shared",
    )(normed, *groups, residual)
    answers = pl.pallas_call(
        expert_kernel,
        out_shape=shape((16, 4, CAP, width), BF16),
        grid=(4,),
        in_specs=[
            pl.BlockSpec((16, None, CAP, width), lambda e: (0, e, 0, 0)),
            pl.BlockSpec((None, width, 512), lambda e: (e, 0, 0)),
            pl.BlockSpec((None, width, 512), lambda e: (e, 0, 0)),
            pl.BlockSpec((None, 512, width), lambda e: (e, 0, 0)),
        ],
        out_specs=pl.BlockSpec((16, None, CAP, width), lambda e: (0, e, 0, 0)),
        name="experts",
    )(received, ex_gate, ex_up, ex_down)
    returned = lax.all_to_all(answers, "seq", split_axis=0, concat_axis=0, tiled=True)
    layer_out = pl.pallas_call(
        leave_kernel,
        out_shape=shape((ROWS, width), BF16),
        in_specs=[VM] * 4,
        out_specs=VM,
        name="leave",
    )(returned.reshape(1024, width), mix_high, mix_low, base)
    return (layer_out, state_cache)


def solution(mesh):
    placed = (
        P(("seq", "exp"), None),
        P(),
        P(None, "exp"),
        P(None, "exp"),
        P(),
        P(None, "exp"),
        P(None, "exp"),
        P(),
        P("exp"),
        P("exp"),
        P("exp"),
        P("exp"),
        P("exp", None),
        P(),
        P(None, "exp"),
        P(None, "exp"),
        P("exp", None),
        P("seq", None, None),
        P("seq", None, None),
        P("seq", None, None),
        P(("seq", "exp"), None),
        P(("seq", "exp"), None),
        P(),
        P(),
    )
    return jax.shard_map(
        body,
        mesh=mesh,
        in_specs=placed,
        out_specs=(P(("seq", "exp"), None), P("seq", "exp", None, None)),
        check_vma=False,
    )
```

```python
import functools

import jax
import jax.numpy as jnp
from jax import lax
from jax.experimental import pallas as pl
from jax.experimental.pallas import tpu as pltpu
from jax.sharding import PartitionSpec as P


EPS = 1e-05
HIGH = lax.Precision.HIGHEST
F32 = jnp.float32
BF16 = jnp.bfloat16
LANES = 128
ROWS = 128
CHUNK = 128
CAP = 16
HEADS = 6
HALF = 64
WIDE = 384
STATE = 128
DI = 3072
VM = pl.BlockSpec(memory_space=pltpu.VMEM)
SM = pl.BlockSpec(memory_space=pltpu.SMEM)
ANY = pl.BlockSpec(memory_space=pl.ANY)
PLUS = [(i, (i + 2) % 8) for i in range(8)]
MINUS = [(i, (i + 6) % 8) for i in range(8)]
MATE = [(i, i ^ 1) for i in range(8)]


def near_core(*arrays):
    return [pltpu.with_memory_space_constraint(a, pltpu.VMEM) for a in arrays]


def far_core(*arrays):
    return [pltpu.with_memory_space_constraint(a, pltpu.HBM) for a in arrays]


def silu(v):
    return v * (1.0 / (1.0 + jnp.exp(-v)))


def ahead(block, distance):
    return lax.ppermute(block, "seq", [(i, i + distance) for i in range(16 - distance)])


def over_exp(block, route):
    return lax.ppermute(block, "exp", route)


def spread(cols):
    rows = cols.shape[0]
    left = lax.broadcasted_iota(jnp.int32, (rows, LANES), 1) < HALF
    parts = []
    for pair in range(HEADS // 2):
        first = jnp.broadcast_to(cols[:, 2 * pair : 2 * pair + 1], (rows, LANES))
        second = jnp.broadcast_to(cols[:, 2 * pair + 1 : 2 * pair + 2], (rows, LANES))
        parts.append(jnp.where(left, first, second))
    return jnp.concatenate(parts, axis=1)


def chip_of(where):
    return where[0] // 2


def core_of(where):
    return lax.rem(where[0], 2)


def tables_kernel(
    seq, lengths, slots, dt_bias, a_log, d_skip, in_dt, conv_x, conv_bc, g_in, g_mix, g_post, x, bc, z,
    w_all, w_dt, bias, rate, skip, taps, seg_ext, seg_row, gain_in, gain_mix, gain_post, meta, sems,
):
    copies = []
    for i, (ref, at, cols) in enumerate(((x, 0, WIDE), (bc, WIDE, 2 * STATE), (z, WIDE + 2 * STATE, WIDE))):
        copies.append(pltpu.make_async_copy(ref, w_all.at[:, at : at + cols], sems.at[i]))
    for copy in copies:
        copy.start()
    base = seq[0] * (8 * CHUNK)
    total = jnp.int32(0)
    ends = []
    for req in range(16):
        total = total + lengths[req]
        ends.append(total)

    lane = lax.broadcasted_iota(jnp.int32, (1, LANES), 1)
    wide = lax.broadcasted_iota(jnp.int32, (1, WIDE), 1)
    bias_row = jnp.zeros((1, LANES), F32)
    rate_row = jnp.zeros((1, LANES), F32)
    skip_row = jnp.zeros((1, WIDE), F32)
    for head in range(HEADS):
        bias_row = jnp.where(lane == head, dt_bias[head], bias_row)
        rate_row = jnp.where(lane == head, a_log[head], rate_row)
        skip_row = jnp.where((wide >= head * HALF) & (wide < (head + 1) * HALF), d_skip[head], skip_row)
    bias[...] = bias_row
    rate[...] = jnp.where(lane < HEADS, jnp.exp(rate_row), 0.0)
    skip[...] = skip_row
    taps[:, :WIDE] = conv_x[...]
    taps[:, WIDE:] = conv_bc[...]
    gain_in[0, :] = g_in[...]
    gain_mix[0, :] = g_mix[...]
    gain_post[0, :] = g_post[...]
    w_dt[...] = jnp.zeros_like(w_dt)
    w_dt[:HEADS, :] = in_dt[...]

    def seg_at(positions):
        found = jnp.zeros_like(positions)
        for end in ends:
            found = found + jnp.where(positions >= end, 1, 0)
        return jnp.where(positions >= 0, found, -1)

    ext_i = lax.broadcasted_iota(jnp.int32, (8 * CHUNK + 16, 1), 0)
    seg_ext[...] = seg_at(base + ext_i - 16)
    row_i = lax.broadcasted_iota(jnp.int32, (8, CHUNK), 0)
    seg_row[...] = seg_at(base + row_i * CHUNK + lax.broadcasted_iota(jnp.int32, (8, CHUNK), 1))
    for c in range(8):
        before = seg_at(base + (c * CHUNK - 1))
        meta[c] = before
        meta[8 + c] = before
        meta[16 + c] = seg_at(base + (c * CHUNK + CHUNK - 1))
        meta[24 + c] = seg_at(base + c * CHUNK)
    first = seg_at(base - 1)
    open_req = jnp.maximum(first, 0)
    open_end, open_slot, source = jnp.int32(0), jnp.int32(0), jnp.int32(0)
    for req in range(16):
        meta[32 + req] = ends[req] - 1 - base
        meta[48 + req] = slots[req]
        open_end = jnp.where(open_req == req, ends[req] - 1 - base, open_end)
        open_slot = jnp.where(open_req == req, slots[req], open_slot)
        source = jnp.where(slots[req] == seq[0], (ends[req] - 1) // (8 * CHUNK), source)
    holds = (first >= 0) & (open_end >= 0) & (open_end < 8 * CHUNK)
    meta[64] = open_slot
    meta[65] = jnp.where(holds, 1, 0)
    meta[66] = jnp.clip(open_end, 0, 8 * CHUNK - 1)
    meta[67] = source
    for copy in copies:
        copy.wait()


def join_kernel(up, down, both, up_low, down_high):
    both[:ROWS, :] = up[...]
    both[ROWS:, :] = down[...]
    up_low[...] = up[:HALF, :]
    down_high[...] = down[HALF:, :]


def project_kernel(where, *refs, plan):
    count = 1 + max(piece[0] for _, pieces in plan for piece in pieces)
    blocks, rest = refs[:count], refs[count:]
    gain, w_all, w_dt, bias, rate = rest[:5]
    conv_out, step_out, cum_out, z_out, normed = rest[-5:]
    chip, core = chip_of(where), core_of(where)
    rows_i = lax.broadcasted_iota(jnp.int32, (CHUNK, CHUNK), 0)
    cols_i = lax.broadcasted_iota(jnp.int32, (CHUNK, CHUNK), 1)
    lower = (rows_i >= cols_i).astype(F32)
    for offset, pieces in plan:
        for index, source, rows, own, to in pieces:
            vals = blocks[index][source : source + rows, :].astype(F32)
            meansq = jnp.mean(vals * vals, axis=-1, keepdims=True)
            place = core if own else 1 - core
            start = pl.multiple_of(place * ROWS + to, HALF)
            normed[pl.ds(start, rows), :] = (vals * lax.rsqrt(meansq + EPS) * gain[...]).astype(BF16)
        rows = normed[...]
        at = pl.multiple_of(lax.rem(chip + offset, 4) * (2 * ROWS), 2 * ROWS)
        here = pl.ds(at, 2 * ROWS)
        raw = lax.dot_general(rows, w_dt[...], (((1,), (1,)), ((), ())), preferred_element_type=F32)
        raw = raw.astype(BF16).astype(F32) + bias[...]
        step = jnp.maximum(raw, 0.0) + jnp.log1p(jnp.exp(-jnp.abs(raw)))
        step_out[here, :] = step
        decay = -step * rate[...]
        for part in (0, 1):
            piece = decay[part * CHUNK : (part + 1) * CHUNK, :]
            cum_out[pl.ds(at + part * CHUNK, CHUNK), :] = jnp.dot(
                lower, piece, precision=HIGH, preferred_element_type=F32
            )
        mixed = jnp.dot(rows, w_all[...], preferred_element_type=F32).astype(BF16)
        conv_out[here, :] = mixed[:, :640]
        z_out[here, :] = silu(mixed[:, 640:].astype(F32))


def conv_chunk(prior, here, seg, w_conv):
    joined = jnp.concatenate([prior, here], axis=0)
    total = here * w_conv[3:4, :]
    own = seg[16:, :]
    for lag in (1, 2, 3):
        kept = (pltpu.roll(seg, lag, 0)[16:, :] == own).astype(F32)
        moved = pltpu.roll(joined, lag, 0)[16:, :]
        total = total + (kept * moved) * w_conv[3 - lag : 4 - lag, :]
    return silu(total).astype(BF16)


def fresh_state(mixed, step, cum, seg, last_seg):
    last = cum[CHUNK - 1 : CHUNK, :]
    tail = jnp.where(seg == last_seg, jnp.exp(last - cum), 0.0)
    drive = mixed[:, :WIDE].astype(F32) * spread(step * tail)
    return lax.dot_general(
        mixed[:, WIDE : WIDE + STATE], drive.astype(BF16), (((0,), (0,)), ((), ())), preferred_element_type=F32
    )


def conv_kernel(meta, conv_in, seg_ext, step, cum, w_conv, x_out, bc_out, fresh_out):
    def chunk(c, carry):
        start = pl.multiple_of(c * CHUNK, CHUNK)
        rows = pl.ds(start, CHUNK)
        seg = seg_ext[pl.ds(start, CHUNK + 16), :]
        prior = conv_in[pl.ds(pl.multiple_of(start - 16, 16), 16), :].astype(F32)
        mixed = conv_chunk(prior, conv_in[rows, :].astype(F32), seg, w_conv)
        x_out[rows, :] = mixed[:, :WIDE]
        bc_out[rows, :] = mixed[:, WIDE:]
        fresh_out[c] = fresh_state(mixed, step[rows, :], cum[rows, :], seg[16:, :], meta[16 + c])
        return carry

    lax.fori_loop(1, 8, chunk, 0)


def row_spread(row):
    return spread(jnp.broadcast_to(row, (8, LANES)))[:1, :]


def chain_kernel(meta, conv_in, edge, seg_ext, step, cum, w_conv, fresh, x_in, bc_in, x_out, bc_out, state_out, send_out, past_out):
    before_dev = meta[0]
    seg = seg_ext[: CHUNK + 16, :]
    mixed = conv_chunk(edge[...].astype(F32), conv_in[:CHUNK, :].astype(F32), seg, w_conv)
    x_out[:CHUNK, :] = mixed[:, :WIDE]
    bc_out[:CHUNK, :] = mixed[:, WIDE:]
    first = fresh_state(mixed, step[:CHUNK, :], cum[:CHUNK, :], seg[16:, :], meta[16])
    held = jnp.zeros((STATE, WIDE), F32)
    past = jnp.zeros((1, LANES), F32)
    for c in range(8):
        last = cum[(c + 1) * CHUNK - 1 : (c + 1) * CHUNK, :]
        state_out[c] = held.astype(BF16)
        past_out[c : c + 1, :] = past
        persist = row_spread(jnp.where(meta[16 + c] == meta[8 + c], jnp.exp(last), 0.0))
        held = persist * held + (first if c == 0 else fresh[c])
        past = past + last
    send_out[:STATE, :] = held.astype(BF16)
    passed = jnp.where(meta[16 + 7] == before_dev, jnp.exp(past), 0.0)
    wide = spread(jnp.broadcast_to(passed, (16, LANES)))
    high = wide.astype(BF16)
    low = (wide - high.astype(F32)).astype(BF16)
    row = lax.broadcasted_iota(jnp.int32, (16, WIDE), 0)
    send_out[STATE:, :] = jnp.where(row == 0, high, low)


def factor_of(message):
    both = message[STATE:, :].astype(F32)
    return both[0:1, :] + both[1:2, :]


def pair_kernel(sent, got, out):
    own_factor, got_factor = factor_of(sent), factor_of(got)
    out[:STATE, :] = (sent[:STATE, :].astype(F32) + own_factor * got[:STATE, :].astype(F32)).astype(BF16)
    wide = jnp.broadcast_to(own_factor * got_factor, (16, WIDE))
    high = wide.astype(BF16)
    low = (wide - high.astype(F32)).astype(BF16)
    row = lax.broadcasted_iota(jnp.int32, (16, WIDE), 0)
    out[STATE:, :] = jnp.where(row == 0, high, low)


def entering_state(near, far):
    return near[:STATE, :].astype(F32) + factor_of(near) * far[:STATE, :].astype(F32)


def open_kernel(meta, near, far, cum, past, ends_in, ends_out):
    at = meta[66]
    total = cum[pl.ds(at, 1), :] + past[pl.ds(at // CHUNK, 1), :]
    hold = row_spread(jnp.where(meta[65] > 0, jnp.exp(total), 0.0))
    value = ends_in[0].astype(F32)
    ends_out[0] = jnp.where(meta[65] > 0, value + hold * entering_state(near, far), value).astype(BF16)


def local_kernel(meta, x_in, bc_in, cum_in, step_in, seg_ext, seg_row, state_in, skip, *rest, first, last):
    y_out = rest[-1]
    rows_i = lax.broadcasted_iota(jnp.int32, (CHUNK, CHUNK), 0)
    cols_i = lax.broadcasted_iota(jnp.int32, (CHUNK, CHUNK), 1)
    causal = rows_i >= cols_i
    left = lax.broadcasted_iota(jnp.int32, (CHUNK, LANES), 1) < HALF

    def chunk(c):
        start = pl.multiple_of(c * CHUNK, CHUNK)
        rows = pl.ds(start, CHUNK)
        x = x_in[rows, :].astype(F32)
        b_rows, c_rows = bc_in[rows, :STATE], bc_in[rows, STATE:]
        cum = cum_in[rows, :]
        cum_t = cum.T
        seg = seg_ext[pl.ds(start + 16, CHUNK), :]
        mask = causal & (seg == seg_row[pl.ds(c, 1), :])
        scores = lax.dot_general(c_rows, b_rows, (((1,), (1,)), ((), ())), preferred_element_type=F32)
        scores = jnp.where(mask, scores, 0.0)
        drive_b = (x * spread(step_in[rows, :])).astype(BF16)
        entry = jnp.where(seg == meta[8 + c], jnp.exp(cum), 0.0)
        carried = jnp.dot(c_rows, state_in[c], preferred_element_type=F32)
        total = spread(entry) * carried + skip[...] * x
        for pair in range(HEADS // 2):
            block = drive_b[:, pair * LANES : (pair + 1) * LANES]
            zero = jnp.zeros_like(block)
            acc = total[:, pair * LANES : (pair + 1) * LANES]
            for side in (0, 1):
                head = 2 * pair + side
                gap = jnp.minimum(cum[:, head : head + 1] - cum_t[head : head + 1, :], 0.0)
                weights = (scores * jnp.exp(gap)).astype(BF16)
                value = jnp.where(left, block, zero) if side == 0 else jnp.where(left, zero, block)
                acc = acc + jnp.dot(weights, value, preferred_element_type=F32)
            y_out[rows, pair * LANES : (pair + 1) * LANES] = acc

    def two_chunks(i, carry):
        chunk(first + 2 * i)
        chunk(first + 2 * i + 1)
        return carry

    lax.fori_loop(0, (last - first) // 2, two_chunks, 0)


def ends_kernel(meta, x_in, bc_in, cum_in, step_in, seg_ext, state_in, ends_out):
    def close(req, carry):
        at = meta[32 + req]

        @pl.when((at >= 0) & (at < 8 * CHUNK))
        def _():
            c = at // CHUNK
            rows = pl.ds(pl.multiple_of(c * CHUNK, CHUNK), CHUNK)
            cum = cum_in[rows, :]
            cum_end = cum_in[pl.ds(at, 1), :]
            seg = seg_ext[pl.ds(c * CHUNK + 16, CHUNK), :]
            weight = jnp.where(seg == req, jnp.exp(jnp.minimum(cum_end - cum, 0.0)), 0.0)
            drive = x_in[rows, :].astype(F32) * spread(step_in[rows, :] * weight)
            fresh = lax.dot_general(
                bc_in[rows, :STATE], drive.astype(BF16), (((0,), (0,)), ((), ())), preferred_element_type=F32
            )
            hold = row_spread(jnp.where(req == meta[8 + c], jnp.exp(cum_end), 0.0))
            ends_out[meta[48 + req]] = (fresh + hold * state_in[c].astype(F32)).astype(BF16)

        return carry

    lax.fori_loop(meta[24], meta[16 + 7] + 1, close, 0)


def out_kernel(where, meta, y_in, bc_in, cum_in, seg_ext, past, z_in, near, far, norm_gain, w_out, *rest, mate):
    gated = rest[-1]
    core = core_of(where)
    if mate:
        core = 1 - core
    state = entering_state(near, far).astype(BF16)
    squares = []
    for rel in range(4):
        block = lax.rem(chip_of(where) + rel, 4) * 2 + core
        start = pl.multiple_of(block * ROWS, ROWS)
        rows = pl.ds(start, ROWS)
        carried = jnp.dot(bc_in[rows, STATE:], state, preferred_element_type=F32)
        seg = seg_ext[pl.ds(start + 16, ROWS), :]
        lead = jnp.where(seg == meta[0], jnp.exp(cum_in[rows, :] + past[pl.ds(block, 1), :]), 0.0)
        g = (y_in[rows, :] + spread(lead) * carried) * z_in[rows, :]
        squares.append(jnp.broadcast_to(jnp.sum(g * g, axis=1, keepdims=True), (ROWS, LANES)))
        gated[rel * ROWS : (rel + 1) * ROWS, :] = (g * norm_gain[...]).astype(BF16)

    if mate:
        (out,) = rest[:-1]
        for pair in (0, 1):
            mixed = jnp.dot(gated[pair * 256 : (pair + 1) * 256, :], w_out[...], preferred_element_type=F32)
            for rel in (2 * pair, 2 * pair + 1):
                at = (rel - 2 * pair) * ROWS
                out[rel, :, :1536] = mixed[at : at + ROWS, :].astype(BF16)
                out[rel, :, 1536:] = squares[rel].astype(BF16)
    else:
        other, send_a, send_b, kept_0, kept_1, kept_3 = rest[:-1]
        places = (
            ((kept_0, 0), (kept_0, HALF)),
            ((kept_1, 0), (send_a, HALF)),
            ((send_a, 0), (send_b, HALF)),
            ((send_b, 0), (kept_3, 0)),
        )
        for pair in (0, 1):
            mixed = jnp.dot(gated[pair * 256 : (pair + 1) * 256, :], w_out[...], preferred_element_type=F32)
            for rel in (2 * pair, 2 * pair + 1):
                at = (rel - 2 * pair) * ROWS
                for side, (ref, to) in enumerate(places[rel]):
                    lo = side * HALF
                    ref[to : to + HALF, :1536] = (
                        mixed[at + lo : at + lo + HALF, :] + other[rel, lo : lo + HALF, :1536].astype(F32)
                    ).astype(BF16)
                    ref[to : to + HALF, 1536:] = (
                        squares[rel][lo : lo + HALF, :] + other[rel, lo : lo + HALF, 1536:].astype(F32)
                    ).astype(BF16)


def enter_kernel(h0, p_a, p_b, q_a, q_b, tokens, gain, spots, residual_out, normed_out, outgoing, held):
    @pl.when(pl.program_id(0) == 0)
    def _():
        first = h0[:HALF, :].astype(F32) + p_b[:HALF, :].astype(F32) + q_a[...].astype(F32)
        second = h0[HALF:, :].astype(F32) + p_a[HALF:, :].astype(F32) + q_b[...].astype(F32)
        both = jnp.concatenate([first, second], axis=0)
        scale = lax.rsqrt(both[:, 1536:1537] * (1.0 / DI) + EPS)
        residual = tokens[...].astype(F32) + both[:, :1536] * scale
        residual_out[...] = residual
        meansq = jnp.mean(residual * residual, axis=-1, keepdims=True)
        normed = (residual * lax.rsqrt(meansq + EPS) * gain[...]).astype(BF16)
        normed_out[...] = normed
        held[...] = normed

    outgoing[...] = jnp.dot(spots[...], held[...], preferred_element_type=F32).astype(BF16)


def expert_kernel(rows_ref, gate, up, down, out, total):
    rows = rows_ref[:, pl.program_id(0)].reshape(256, 1536)
    g = jnp.dot(rows, gate[...], preferred_element_type=F32)
    u = jnp.dot(rows, up[...], preferred_element_type=F32)
    hidden = (silu(g) * u).astype(BF16)
    term = jnp.dot(hidden, down[...], preferred_element_type=F32)

    @pl.when(pl.program_id(1) == 0)
    def _():
        total[...] = term

    @pl.when(pl.program_id(1) == 1)
    def _():
        out[...] = (total[...] + term).astype(BF16).reshape(16, CAP, 1536)


def shared_kernel(rows_ref, w0, w1, w2, w3, w4, w5, w6, w7, residual, out):
    rows = rows_ref[...]
    total = residual[...]
    for w in (w0, w1, w2, w3, w4, w5, w6, w7):
        both = lax.dot_general(rows, w[:256, :], (((1,), (1,)), ((), ())), preferred_element_type=F32)
        hidden = (silu(both[:, :128]) * both[:, 128:]).astype(BF16)
        total = total + jnp.dot(hidden, w[256:, :], preferred_element_type=F32)
    out[...] = total


def leave_kernel(returned, mix, base, out):
    out[...] = (base[...] + jnp.dot(mix[...], returned[...], preferred_element_type=F32)).astype(BF16)


def vmem(dims, dtype):
    return pltpu.VMEM(dims, dtype)


def hbm(dims, dtype):
    return pltpu.HBM(dims, dtype)


def limit(mib):
    return pltpu.CompilerParams(vmem_limit_bytes=mib << 20)


def shape(dims, dtype):
    return jax.ShapeDtypeStruct(dims, dtype)


def body(
    tokens,
    in_gain,
    in_z,
    in_x,
    in_bc,
    in_dt,
    conv_x,
    conv_bc,
    dt_bias,
    a_log,
    d_skip,
    norm_gain,
    out_w,
    post_gain,
    sh_gate,
    sh_up,
    sh_down,
    ex_gate,
    ex_up,
    ex_down,
    routes,
    gates,
    lengths,
    cache_slot,
):
    seq_idx = lax.axis_index("seq")
    exp_idx = lax.axis_index("exp")
    where_am_i = jnp.reshape(exp_idx, (1,)).astype(jnp.int32)
    width = tokens.shape[1]
    row_count = 8 * ROWS

    up = over_exp(tokens, PLUS)
    down = over_exp(tokens, MINUS)
    mate = over_exp(tokens, MATE)

    (w_all, w_dt, bias, rate, skip, taps, seg_ext, seg_row, gain_in, gain_mix, gain_post, meta) = pl.pallas_call(
        tables_kernel,
        out_shape=(
            vmem((width, 1024), BF16),
            vmem((LANES, width), BF16),
            vmem((1, LANES), F32),
            vmem((1, LANES), F32),
            vmem((1, WIDE), F32),
            vmem((4, 640), F32),
            vmem((row_count + 16, 1), jnp.int32),
            vmem((8, CHUNK), jnp.int32),
            vmem((1, width), F32),
            vmem((1, WIDE), F32),
            vmem((1, width), F32),
            shape((80,), jnp.int32),
        ),
        in_specs=[SM] * 6 + [VM] * 6 + [ANY] * 3,
        out_specs=(VM,) * 11 + (SM,),
        scratch_shapes=[pltpu.SemaphoreType.DMA((3,))],
        compiler_params=limit(16),
        name="tables",
    )(
        seq_idx.reshape(1).astype(jnp.int32),
        lengths,
        cache_slot,
        dt_bias,
        a_log,
        d_skip,
        in_dt.T,
        conv_x,
        conv_bc,
        in_gain,
        norm_gain,
        post_gain,
        *far_core(in_x, in_bc, in_z),
    )

    picks = (routes[:, :, None] == jnp.arange(64, dtype=jnp.int32)).astype(F32)
    named = jnp.sum(picks, axis=1)
    weight = jnp.sum(picks * gates[:, :, None], axis=1)
    earlier = (jnp.arange(ROWS)[:, None] > jnp.arange(ROWS)[None, :]).astype(BF16)
    rank = jnp.dot(earlier, named.astype(BF16), preferred_element_type=F32)
    rank = jnp.where(named > 0, rank, -1.0)
    slots = jnp.arange(1024, dtype=jnp.int32)
    fan = (slots[None, :] // CAP == jnp.arange(64, dtype=jnp.int32)[:, None]).astype(BF16)
    rank_wide = jnp.dot(rank.astype(BF16), fan, preferred_element_type=F32)
    hit = rank_wide == (slots % CAP).astype(F32)[None, :]
    w_high = weight.astype(BF16)
    mix = jnp.where(hit, jnp.dot(w_high, fan, preferred_element_type=F32), 0.0).astype(BF16)
    spots = hit.astype(BF16).T

    def project(plan, blocks, *done):
        return pl.pallas_call(
            functools.partial(project_kernel, plan=plan),
            out_shape=(
                vmem((row_count, 640), BF16),
                vmem((row_count, LANES), F32),
                vmem((row_count, LANES), F32),
                vmem((row_count, WIDE), F32),
            ),
            in_specs=[SM] + [VM] * (len(blocks) + 5 + len(done)),
            out_specs=(VM,) * 4,
            scratch_shapes=[pltpu.VMEM((2 * ROWS, width), BF16)],
            input_output_aliases={len(blocks) + 6 + i: i for i in range(len(done))},
            compiler_params=limit(16),
            name="project",
        )(where_am_i, *near_core(*blocks, gain_in, w_all, w_dt, bias, rate, *done))

    done = project(((0, ((0, 0, ROWS, True, 0), (1, 0, ROWS, False, 0))),), (tokens, mate))
    up, down, done = lax.optimization_barrier((up, down, done))
    both, up_low, down_high = pl.pallas_call(
        join_kernel,
        out_shape=(
            vmem((2 * ROWS, width), BF16),
            vmem((HALF, width), BF16),
            vmem((HALF, width), BF16),
        ),
        in_specs=[VM] * 2,
        out_specs=(VM,) * 3,
        compiler_params=limit(16),
        name="join",
    )(*near_core(up, down))
    far_a = over_exp(up_low, PLUS)
    far_b = over_exp(down_high, MINUS)
    both_mate = over_exp(both, MATE)
    done = project(
        (
            (3, ((0, 0, ROWS, True, 0), (1, 0, ROWS, False, 0))),
            (1, ((0, ROWS, ROWS, True, 0), (1, ROWS, ROWS, False, 0))),
        ),
        (both, both_mate),
        *done,
    )
    far_a, far_b, done = lax.optimization_barrier((far_a, far_b, done))
    conv_in, step, cum, z = project(
        ((2, ((0, 0, HALF, True, 0), (1, 0, HALF, True, HALF), (2, 0, HALF, False, 0), (3, 0, HALF, False, HALF))),),
        (far_a, far_b, over_exp(far_a, MATE), over_exp(far_b, MATE)),
        *done,
    )

    edge = ahead(conv_in[row_count - 16 :], 1)
    x_rows, bc_rows, fresh = pl.pallas_call(
        conv_kernel,
        out_shape=(
            vmem((row_count, WIDE), BF16),
            vmem((row_count, 2 * STATE), BF16),
            vmem((8, STATE, WIDE), F32),
        ),
        in_specs=[SM] + [VM] * 5,
        out_specs=(VM,) * 3,
        compiler_params=limit(16),
        name="conv",
    )(meta, *near_core(conv_in, seg_ext, step, cum, taps))
    x_rows, bc_rows, states, sent, past = pl.pallas_call(
        chain_kernel,
        out_shape=(
            vmem((row_count, WIDE), BF16),
            vmem((row_count, 2 * STATE), BF16),
            vmem((8, STATE, WIDE), BF16),
            vmem((STATE + 16, WIDE), BF16),
            vmem((8, LANES), F32),
        ),
        in_specs=[SM] + [VM] * 9,
        out_specs=(VM,) * 5,
        input_output_aliases={8: 0, 9: 1},
        compiler_params=limit(16),
        name="chain",
    )(meta, *near_core(conv_in, edge, seg_ext, step, cum, taps, fresh, x_rows, bc_rows))

    def local_part(first, last, *done):
        return pl.pallas_call(
            functools.partial(local_kernel, first=first, last=last),
            out_shape=vmem((row_count, WIDE), F32),
            in_specs=[SM] + [VM] * (8 + len(done)),
            out_specs=VM,
            input_output_aliases={9: 0} if done else {},
            compiler_params=limit(16),
            name="local",
        )(meta, *near_core(x_rows, bc_rows, cum, step, seg_ext, seg_row, states, skip, *done))

    got = ahead(sent, 1)
    y_local = local_part(0, 4)
    got, y_local = lax.optimization_barrier((got, y_local))
    two = pl.pallas_call(
        pair_kernel,
        out_shape=vmem((STATE + 16, WIDE), BF16),
        in_specs=[VM, VM],
        out_specs=VM,
        compiler_params=limit(16),
        name="pair",
    )(*near_core(sent, got))
    two, y_local = lax.optimization_barrier((two, y_local))
    near = ahead(two, 1)
    far = ahead(two, 3)
    y_local = local_part(4, 8, y_local)
    near, far, y_local, states = lax.optimization_barrier((near, far, y_local, states))

    def project_out(mate, *other):
        wide = width + LANES
        if mate:
            outs = vmem((4, ROWS, wide), BF16)
        else:
            outs = tuple(vmem((rows, wide), BF16) for rows in (ROWS, ROWS, ROWS, HALF, HALF))
        return pl.pallas_call(
            functools.partial(out_kernel, mate=mate),
            out_shape=outs,
            in_specs=[SM, SM] + [VM] * (10 + len(other)),
            out_specs=VM if mate else (VM,) * 5,
            scratch_shapes=[pltpu.VMEM((4 * ROWS, WIDE), BF16)],
            compiler_params=limit(16),
            name="out_mate" if mate else "out_own",
        )(
            where_am_i,
            meta,
            *near_core(y_local, bc_rows, cum, seg_ext, past, z, near, far, gain_mix, out_w, *other),
        )

    mate_part = project_out(True)
    swapped = over_exp(mate_part, MATE)

    mate_part, states = lax.optimization_barrier((mate_part, states))
    ends_local = pl.pallas_call(
        ends_kernel,
        out_shape=shape((16, STATE, WIDE), BF16),
        in_specs=[SM] + [VM] * 6,
        out_specs=VM,
        compiler_params=limit(16),
        name="ends",
    )(meta, *near_core(x_rows, bc_rows, cum, step, seg_ext, states))
    slot_block = pl.BlockSpec((1, STATE, WIDE), lambda i, meta: (meta[64], 0, 0))
    ends_local = pl.pallas_call(
        open_kernel,
        out_shape=shape((16, STATE, WIDE), BF16),
        grid_spec=pltpu.PrefetchScalarGridSpec(
            num_scalar_prefetch=1,
            grid=(1,),
            in_specs=[VM] * 4 + [slot_block],
            out_specs=slot_block,
        ),
        input_output_aliases={5: 0},
        compiler_params=limit(16),
        name="open",
    )(meta, *near_core(near, far, cum, past), ends_local)
    send_a, send_b, kept_0, kept_1, kept_3 = project_out(False, swapped)
    send_a, send_b, ends_local = lax.optimization_barrier((send_a, send_b, ends_local))
    p_a = over_exp(send_a, PLUS)
    p_b = over_exp(send_b, MINUS)
    ends_all = lax.all_to_all(ends_local, "seq", split_axis=0, concat_axis=0, tiled=True)
    q_a = over_exp((kept_1.astype(F32) + p_a[:HALF].astype(F32)).astype(BF16), PLUS)
    q_b = over_exp((kept_3.astype(F32) + p_b[HALF:].astype(F32)).astype(BF16), MINUS)

    residual, normed, outgoing = pl.pallas_call(
        enter_kernel,
        out_shape=(hbm((ROWS, width), F32), hbm((ROWS, width), BF16), hbm((1024, width), BF16)),
        grid=(4,),
        in_specs=[VM] * 7 + [pl.BlockSpec((256, ROWS), lambda i: (i, 0))],
        out_specs=(VM, VM, pl.BlockSpec((256, width), lambda i: (i, 0))),
        scratch_shapes=[pltpu.VMEM((ROWS, width), BF16)],
        compiler_params=limit(16),
        name="enter",
    )(*near_core(kept_0, p_a, p_b, q_a, q_b, tokens, gain_post), spots)
    received = lax.all_to_all(
        outgoing.reshape(16, 4, CAP, width), "seq", split_axis=0, concat_axis=0, tiled=True
    )
    sh_gate, sh_up, sh_down, ends_all, outgoing = lax.optimization_barrier(
        (sh_gate, sh_up, sh_down, ends_all, outgoing)
    )
    final = lax.dynamic_index_in_dim(ends_all, meta[67], 0, False).astype(F32)
    state_cache = final.T.reshape(1, HEADS, HALF, STATE)
    packed = jnp.concatenate([sh_gate.T, sh_up.T, sh_down])
    half = packed.shape[0] // 2
    g_up = over_exp(packed, PLUS)
    g_down = over_exp(packed, MINUS)
    g_mate = over_exp(packed, MATE)
    received, g_up, g_down, g_mate, state_cache = lax.optimization_barrier(
        (received, g_up, g_down, g_mate, state_cache)
    )
    answers = pl.pallas_call(
        expert_kernel,
        out_shape=hbm((16, 4, CAP, width), BF16),
        grid=(4, 2),
        in_specs=[
            VM,
            pl.BlockSpec((None, width, 256), lambda e, f: (e, 0, f)),
            pl.BlockSpec((None, width, 256), lambda e, f: (e, 0, f)),
            pl.BlockSpec((None, 256, width), lambda e, f: (e, f, 0)),
        ],
        out_specs=pl.BlockSpec((16, None, CAP, width), lambda e, f: (0, e, 0, 0)),
        scratch_shapes=[pltpu.VMEM((256, width), F32)],
        compiler_params=limit(20),
        name="experts",
    )(*near_core(received), *far_core(ex_gate, ex_up, ex_down))
    returned = lax.all_to_all(answers, "seq", split_axis=0, concat_axis=0, tiled=True)
    g_up, g_down, answers = lax.optimization_barrier((g_up, g_down, answers))
    g_far = jnp.concatenate([over_exp(g_up[:half], PLUS), over_exp(g_down[half:], MINUS)])
    groups = (packed, g_mate, g_up, over_exp(g_up, MATE), g_down, over_exp(g_down, MATE), g_far, over_exp(g_far, MATE))
    base = pl.pallas_call(
        shared_kernel,
        out_shape=hbm((ROWS, width), F32),
        in_specs=[VM] * 10,
        out_specs=VM,
        compiler_params=limit(16),
        name="shared",
    )(normed, *groups, residual)
    layer_out = pl.pallas_call(
        leave_kernel,
        out_shape=shape((ROWS, width), BF16),
        in_specs=[VM] * 3,
        out_specs=VM,
        compiler_params=limit(16),
        name="leave",
    )(*near_core(returned.reshape(1024, width), mix), *far_core(base))
    return (layer_out, state_cache)


def solution(mesh):
    placed = (
        P(("seq", "exp"), None),
        P(),
        P(None, "exp"),
        P(None, "exp"),
        P(),
        P(None, "exp"),
        P(None, "exp"),
        P(),
        P("exp"),
        P("exp"),
        P("exp"),
        P("exp"),
        P("exp", None),
        P(),
        P(None, "exp"),
        P(None, "exp"),
        P("exp", None),
        P("seq", None, None),
        P("seq", None, None),
        P("seq", None, None),
        P(("seq", "exp"), None),
        P(("seq", "exp"), None),
        P(),
        P(),
    )
    return jax.shard_map(
        body,
        mesh=mesh,
        in_specs=placed,
        out_specs=(P(("seq", "exp"), None), P("seq", "exp", None, None)),
        check_vma=False,
    )
```

```python
import functools

import jax
import jax.numpy as jnp
from jax import lax
from jax.experimental import pallas as pl
from jax.experimental.pallas import tpu as pltpu
from jax.sharding import PartitionSpec as P


EPS = 1e-05
HIGH = lax.Precision.HIGHEST
F32 = jnp.float32
BF16 = jnp.bfloat16
LANES = 128
ROWS = 128
CHUNK = 128
CAP = 16
HEADS = 6
HALF = 64
WIDE = 384
STATE = 128
DI = 3072
VM = pl.BlockSpec(memory_space=pltpu.VMEM)
SM = pl.BlockSpec(memory_space=pltpu.SMEM)
ANY = pl.BlockSpec(memory_space=pl.ANY)
PLUS = [(i, (i + 2) % 8) for i in range(8)]
MINUS = [(i, (i + 6) % 8) for i in range(8)]
MATE = [(i, i ^ 1) for i in range(8)]


def near_core(*arrays):
    return [pltpu.with_memory_space_constraint(a, pltpu.VMEM) for a in arrays]


def far_core(*arrays):
    return [pltpu.with_memory_space_constraint(a, pltpu.HBM) for a in arrays]


def silu(v):
    return v * (1.0 / (1.0 + jnp.exp(-v)))


def ahead(block, distance):
    return lax.ppermute(block, "seq", [(i, i + distance) for i in range(16 - distance)])


def over_exp(block, route):
    return lax.ppermute(block, "exp", route)


def spread(cols):
    rows = cols.shape[0]
    left = lax.broadcasted_iota(jnp.int32, (rows, LANES), 1) < HALF
    parts = []
    for pair in range(HEADS // 2):
        first = jnp.broadcast_to(cols[:, 2 * pair : 2 * pair + 1], (rows, LANES))
        second = jnp.broadcast_to(cols[:, 2 * pair + 1 : 2 * pair + 2], (rows, LANES))
        parts.append(jnp.where(left, first, second))
    return jnp.concatenate(parts, axis=1)


def chip_of(where):
    return where[0] // 2


def core_of(where):
    return lax.rem(where[0], 2)


def tables_kernel(
    seq, lengths, slots, dt_bias, a_log, d_skip, in_dt, conv_x, conv_bc, g_in, g_mix, g_post, x, bc, z,
    w_all, w_dt, bias, rate, skip, taps, seg_ext, seg_row, gain_in, gain_mix, gain_post, meta, sems,
):
    copies = []
    for i, (ref, at, cols) in enumerate(((x, 0, WIDE), (bc, WIDE, 2 * STATE), (z, WIDE + 2 * STATE, WIDE))):
        copies.append(pltpu.make_async_copy(ref, w_all.at[:, at : at + cols], sems.at[i]))
    for copy in copies:
        copy.start()
    base = seq[0] * (8 * CHUNK)
    total = jnp.int32(0)
    ends = []
    for req in range(16):
        total = total + lengths[req]
        ends.append(total)

    lane = lax.broadcasted_iota(jnp.int32, (1, LANES), 1)
    wide = lax.broadcasted_iota(jnp.int32, (1, WIDE), 1)
    bias_row = jnp.zeros((1, LANES), F32)
    rate_row = jnp.zeros((1, LANES), F32)
    skip_row = jnp.zeros((1, WIDE), F32)
    for head in range(HEADS):
        bias_row = jnp.where(lane == head, dt_bias[head], bias_row)
        rate_row = jnp.where(lane == head, a_log[head], rate_row)
        skip_row = jnp.where((wide >= head * HALF) & (wide < (head + 1) * HALF), d_skip[head], skip_row)
    bias[...] = bias_row
    rate[...] = jnp.where(lane < HEADS, jnp.exp(rate_row), 0.0)
    skip[...] = skip_row
    taps[:, :WIDE] = conv_x[...]
    taps[:, WIDE:] = conv_bc[...]
    gain_in[0, :] = g_in[...]
    gain_mix[0, :] = g_mix[...]
    gain_post[0, :] = g_post[...]
    w_dt[...] = jnp.zeros_like(w_dt)
    w_dt[:HEADS, :] = in_dt[...]

    def seg_at(positions):
        found = jnp.zeros_like(positions)
        for end in ends:
            found = found + jnp.where(positions >= end, 1, 0)
        return jnp.where(positions >= 0, found, -1)

    ext_i = lax.broadcasted_iota(jnp.int32, (8 * CHUNK + 16, 1), 0)
    seg_ext[...] = seg_at(base + ext_i - 16)
    row_i = lax.broadcasted_iota(jnp.int32, (8, CHUNK), 0)
    seg_row[...] = seg_at(base + row_i * CHUNK + lax.broadcasted_iota(jnp.int32, (8, CHUNK), 1))
    for c in range(8):
        before = seg_at(base + (c * CHUNK - 1))
        meta[c] = before
        meta[8 + c] = before
        meta[16 + c] = seg_at(base + (c * CHUNK + CHUNK - 1))
        meta[24 + c] = seg_at(base + c * CHUNK)
    source = jnp.int32(0)
    for req in range(16):
        meta[32 + req] = ends[req] - 1 - base
        meta[48 + req] = slots[req]
        source = jnp.where(slots[req] == seq[0], (ends[req] - 1) // (8 * CHUNK), source)
    meta[64] = source
    for copy in copies:
        copy.wait()


def join_kernel(up, down, both, up_low, down_high):
    both[:ROWS, :] = up[...]
    both[ROWS:, :] = down[...]
    up_low[...] = up[:HALF, :]
    down_high[...] = down[HALF:, :]


def project_kernel(where, *refs, plan):
    count = 1 + max(piece[0] for _, pieces in plan for piece in pieces)
    blocks, rest = refs[:count], refs[count:]
    gain, w_all, w_dt, bias, rate = rest[:5]
    conv_out, step_out, cum_out, z_out, normed = rest[-5:]
    chip, core = chip_of(where), core_of(where)
    rows_i = lax.broadcasted_iota(jnp.int32, (CHUNK, CHUNK), 0)
    cols_i = lax.broadcasted_iota(jnp.int32, (CHUNK, CHUNK), 1)
    lower = (rows_i >= cols_i).astype(F32)
    for offset, pieces in plan:
        for index, source, rows, own, to in pieces:
            vals = blocks[index][source : source + rows, :].astype(F32)
            meansq = jnp.mean(vals * vals, axis=-1, keepdims=True)
            place = core if own else 1 - core
            start = pl.multiple_of(place * ROWS + to, HALF)
            normed[pl.ds(start, rows), :] = (vals * lax.rsqrt(meansq + EPS) * gain[...]).astype(BF16)
        rows = normed[...]
        at = pl.multiple_of(lax.rem(chip + offset, 4) * (2 * ROWS), 2 * ROWS)
        here = pl.ds(at, 2 * ROWS)
        raw = lax.dot_general(rows, w_dt[...], (((1,), (1,)), ((), ())), preferred_element_type=F32)
        raw = raw.astype(BF16).astype(F32) + bias[...]
        step = jnp.maximum(raw, 0.0) + jnp.log1p(jnp.exp(-jnp.abs(raw)))
        step_out[here, :] = step
        decay = -step * rate[...]
        for part in (0, 1):
            piece = decay[part * CHUNK : (part + 1) * CHUNK, :]
            cum_out[pl.ds(at + part * CHUNK, CHUNK), :] = jnp.dot(
                lower, piece, precision=HIGH, preferred_element_type=F32
            )
        mixed = jnp.dot(rows, w_all[...], preferred_element_type=F32).astype(BF16)
        conv_out[here, :] = mixed[:, :640]
        z_out[here, :] = silu(mixed[:, 640:].astype(F32))


def conv_chunk(prior, here, seg, w_conv):
    joined = jnp.concatenate([prior, here], axis=0)
    total = here * w_conv[3:4, :]
    own = seg[16:, :]
    for lag in (1, 2, 3):
        kept = (pltpu.roll(seg, lag, 0)[16:, :] == own).astype(F32)
        moved = pltpu.roll(joined, lag, 0)[16:, :]
        total = total + (kept * moved) * w_conv[3 - lag : 4 - lag, :]
    return silu(total).astype(BF16)


def fresh_state(mixed, step, cum, seg, last_seg):
    last = cum[CHUNK - 1 : CHUNK, :]
    tail = jnp.where(seg == last_seg, jnp.exp(last - cum), 0.0)
    drive = mixed[:, :WIDE].astype(F32) * spread(step * tail)
    return lax.dot_general(
        mixed[:, WIDE : WIDE + STATE], drive.astype(BF16), (((0,), (0,)), ((), ())), preferred_element_type=F32
    )


def conv_kernel(meta, conv_in, seg_ext, step, cum, w_conv, x_out, bc_out, fresh_out):
    for c in range(1, 8):
        start = c * CHUNK
        rows = pl.ds(start, CHUNK)
        seg = seg_ext[pl.ds(start, CHUNK + 16), :]
        prior = conv_in[pl.ds(start - 16, 16), :].astype(F32)
        mixed = conv_chunk(prior, conv_in[rows, :].astype(F32), seg, w_conv)
        x_out[rows, :] = mixed[:, :WIDE]
        bc_out[rows, :] = mixed[:, WIDE:]
        fresh_out[c] = fresh_state(mixed, step[rows, :], cum[rows, :], seg[16:, :], meta[16 + c])


def row_spread(row):
    return spread(jnp.broadcast_to(row, (8, LANES)))[:1, :]


def chain_kernel(meta, conv_in, edge, seg_ext, step, cum, w_conv, fresh, x_in, bc_in, x_out, bc_out, state_out, send_out, past_out):
    before_dev = meta[0]
    seg = seg_ext[: CHUNK + 16, :]
    mixed = conv_chunk(edge[...].astype(F32), conv_in[:CHUNK, :].astype(F32), seg, w_conv)
    x_out[:CHUNK, :] = mixed[:, :WIDE]
    bc_out[:CHUNK, :] = mixed[:, WIDE:]
    first = fresh_state(mixed, step[:CHUNK, :], cum[:CHUNK, :], seg[16:, :], meta[16])
    held = jnp.zeros((STATE, WIDE), F32)
    past = jnp.zeros((1, LANES), F32)
    for c in range(8):
        last = cum[(c + 1) * CHUNK - 1 : (c + 1) * CHUNK, :]
        state_out[c] = held.astype(BF16)
        past_out[c : c + 1, :] = past
        persist = row_spread(jnp.where(meta[16 + c] == meta[8 + c], jnp.exp(last), 0.0))
        held = persist * held + (first if c == 0 else fresh[c])
        past = past + last
    send_out[:STATE, :] = held.astype(BF16)
    passed = jnp.where(meta[16 + 7] == before_dev, jnp.exp(past), 0.0)
    wide = spread(jnp.broadcast_to(passed, (16, LANES)))
    high = wide.astype(BF16)
    low = (wide - high.astype(F32)).astype(BF16)
    row = lax.broadcasted_iota(jnp.int32, (16, WIDE), 0)
    send_out[STATE:, :] = jnp.where(row == 0, high, low)


def factor_of(message):
    both = message[STATE:, :].astype(F32)
    return both[0:1, :] + both[1:2, :]


def pair_kernel(sent, got, out):
    own_factor, got_factor = factor_of(sent), factor_of(got)
    out[:STATE, :] = (sent[:STATE, :].astype(F32) + own_factor * got[:STATE, :].astype(F32)).astype(BF16)
    wide = jnp.broadcast_to(own_factor * got_factor, (16, WIDE))
    high = wide.astype(BF16)
    low = (wide - high.astype(F32)).astype(BF16)
    row = lax.broadcasted_iota(jnp.int32, (16, WIDE), 0)
    out[STATE:, :] = jnp.where(row == 0, high, low)


def entering_state(near, far):
    return near[:STATE, :].astype(F32) + factor_of(near) * far[:STATE, :].astype(F32)


def local_kernel(meta, x_in, bc_in, cum_in, step_in, seg_ext, seg_row, state_in, skip, *rest, first, last):
    y_out = rest[-1]
    rows_i = lax.broadcasted_iota(jnp.int32, (CHUNK, CHUNK), 0)
    cols_i = lax.broadcasted_iota(jnp.int32, (CHUNK, CHUNK), 1)
    causal = rows_i >= cols_i
    left = lax.broadcasted_iota(jnp.int32, (CHUNK, LANES), 1) < HALF

    def chunk(c):
        start = c * CHUNK
        rows = pl.ds(start, CHUNK)
        x = x_in[rows, :].astype(F32)
        b_rows, c_rows = bc_in[rows, :STATE], bc_in[rows, STATE:]
        cum = cum_in[rows, :]
        cum_t = cum.T
        seg = seg_ext[pl.ds(start + 16, CHUNK), :]
        mask = causal & (seg == seg_row[pl.ds(c, 1), :])
        scores = lax.dot_general(c_rows, b_rows, (((1,), (1,)), ((), ())), preferred_element_type=F32)
        scores = jnp.where(mask, scores, 0.0)
        drive_b = (x * spread(step_in[rows, :])).astype(BF16)
        entry = jnp.where(seg == meta[8 + c], jnp.exp(cum), 0.0)
        carried = jnp.dot(c_rows, state_in[c], preferred_element_type=F32)
        total = spread(entry) * carried + skip[...] * x
        for pair in range(HEADS // 2):
            block = drive_b[:, pair * LANES : (pair + 1) * LANES]
            zero = jnp.zeros_like(block)
            acc = total[:, pair * LANES : (pair + 1) * LANES]
            for side in (0, 1):
                head = 2 * pair + side
                gap = jnp.minimum(cum[:, head : head + 1] - cum_t[head : head + 1, :], 0.0)
                weights = (scores * jnp.exp(gap)).astype(BF16)
                value = jnp.where(left, block, zero) if side == 0 else jnp.where(left, zero, block)
                acc = acc + jnp.dot(weights, value, preferred_element_type=F32)
            y_out[rows, pair * LANES : (pair + 1) * LANES] = acc

    for c in range(first, last):
        chunk(c)


def ends_kernel(meta, x_in, bc_in, cum_in, step_in, seg_ext, state_in, near, far, past, ends_out):
    def close(req, carry):
        at = meta[32 + req]

        @pl.when((at >= 0) & (at < 8 * CHUNK))
        def _():
            c = at // CHUNK
            rows = pl.ds(pl.multiple_of(c * CHUNK, CHUNK), CHUNK)
            cum = cum_in[rows, :]
            cum_end = cum_in[pl.ds(at, 1), :]
            seg = seg_ext[pl.ds(c * CHUNK + 16, CHUNK), :]
            weight = jnp.where(seg == req, jnp.exp(jnp.minimum(cum_end - cum, 0.0)), 0.0)
            drive = x_in[rows, :].astype(F32) * spread(step_in[rows, :] * weight)
            fresh = lax.dot_general(
                bc_in[rows, :STATE], drive.astype(BF16), (((0,), (0,)), ((), ())), preferred_element_type=F32
            )
            hold = row_spread(jnp.where(req == meta[8 + c], jnp.exp(cum_end), 0.0))
            since = cum_end + past[pl.ds(c, 1), :]
            opened = row_spread(jnp.where(req == meta[0], jnp.exp(since), 0.0))
            value = fresh + hold * state_in[c].astype(F32) + opened * entering_state(near, far)
            ends_out[meta[48 + req]] = value.astype(BF16)

        return carry

    lax.fori_loop(meta[24], meta[16 + 7] + 1, close, 0)


def out_kernel(where, meta, y_in, bc_in, cum_in, seg_ext, past, z_in, near, far, norm_gain, w_out, *rest, mate):
    gated = rest[-1]
    core = core_of(where)
    if mate:
        core = 1 - core
    state = entering_state(near, far).astype(BF16)
    squares = []
    for rel in range(4):
        block = lax.rem(chip_of(where) + rel, 4) * 2 + core
        start = pl.multiple_of(block * ROWS, ROWS)
        rows = pl.ds(start, ROWS)
        carried = jnp.dot(bc_in[rows, STATE:], state, preferred_element_type=F32)
        seg = seg_ext[pl.ds(start + 16, ROWS), :]
        lead = jnp.where(seg == meta[0], jnp.exp(cum_in[rows, :] + past[pl.ds(block, 1), :]), 0.0)
        g = (y_in[rows, :] + spread(lead) * carried) * z_in[rows, :]
        squares.append(jnp.broadcast_to(jnp.sum(g * g, axis=1, keepdims=True), (ROWS, LANES)))
        gated[rel * ROWS : (rel + 1) * ROWS, :] = (g * norm_gain[...]).astype(BF16)

    if mate:
        (out,) = rest[:-1]
        for pair in (0, 1):
            mixed = jnp.dot(gated[pair * 256 : (pair + 1) * 256, :], w_out[...], preferred_element_type=F32)
            for rel in (2 * pair, 2 * pair + 1):
                at = (rel - 2 * pair) * ROWS
                out[rel, :, :1536] = mixed[at : at + ROWS, :].astype(BF16)
                out[rel, :, 1536:] = squares[rel].astype(BF16)
    else:
        other, send_a, send_b, kept_0, kept_1, kept_3 = rest[:-1]
        places = (
            ((kept_0, 0), (kept_0, HALF)),
            ((kept_1, 0), (send_a, HALF)),
            ((send_a, 0), (send_b, HALF)),
            ((send_b, 0), (kept_3, 0)),
        )
        for pair in (0, 1):
            mixed = jnp.dot(gated[pair * 256 : (pair + 1) * 256, :], w_out[...], preferred_element_type=F32)
            for rel in (2 * pair, 2 * pair + 1):
                at = (rel - 2 * pair) * ROWS
                for side, (ref, to) in enumerate(places[rel]):
                    lo = side * HALF
                    ref[to : to + HALF, :1536] = (
                        mixed[at + lo : at + lo + HALF, :] + other[rel, lo : lo + HALF, :1536].astype(F32)
                    ).astype(BF16)
                    ref[to : to + HALF, 1536:] = (
                        squares[rel][lo : lo + HALF, :] + other[rel, lo : lo + HALF, 1536:].astype(F32)
                    ).astype(BF16)


def enter_kernel(h0, p_a, p_b, q_a, q_b, tokens, gain, spots, residual_out, normed_out, outgoing, held):
    @pl.when(pl.program_id(0) == 0)
    def _():
        first = h0[:HALF, :].astype(F32) + p_b[:HALF, :].astype(F32) + q_a[...].astype(F32)
        second = h0[HALF:, :].astype(F32) + p_a[HALF:, :].astype(F32) + q_b[...].astype(F32)
        both = jnp.concatenate([first, second], axis=0)
        scale = lax.rsqrt(both[:, 1536:1537] * (1.0 / DI) + EPS)
        residual = tokens[...].astype(F32) + both[:, :1536] * scale
        residual_out[...] = residual
        meansq = jnp.mean(residual * residual, axis=-1, keepdims=True)
        normed = (residual * lax.rsqrt(meansq + EPS) * gain[...]).astype(BF16)
        normed_out[...] = normed
        held[...] = normed

    outgoing[...] = jnp.dot(spots[...], held[...], preferred_element_type=F32).astype(BF16)


def expert_kernel(rows_ref, gate, up, down, out):
    rows = rows_ref[:, pl.program_id(0)].reshape(256, 1536)
    g = jnp.dot(rows, gate[...], preferred_element_type=F32)
    u = jnp.dot(rows, up[...], preferred_element_type=F32)
    hidden = (silu(g) * u).astype(BF16)
    out[...] = jnp.dot(hidden, down[...], preferred_element_type=F32).astype(BF16).reshape(16, CAP, 1536)


def shared_kernel(rows_ref, w0, w1, w2, w3, w4, w5, w6, w7, residual, out):
    rows = rows_ref[...]
    total = residual[...]
    for w in (w0, w1, w2, w3, w4, w5, w6, w7):
        both = lax.dot_general(rows, w[:256, :], (((1,), (1,)), ((), ())), preferred_element_type=F32)
        hidden = (silu(both[:, :128]) * both[:, 128:]).astype(BF16)
        total = total + jnp.dot(hidden, w[256:, :], preferred_element_type=F32)
    out[...] = total


def leave_kernel(returned, mix, base, out):
    out[...] = (base[...] + jnp.dot(mix[...], returned[...], preferred_element_type=F32)).astype(BF16)


def vmem(dims, dtype):
    return pltpu.VMEM(dims, dtype)


def hbm(dims, dtype):
    return pltpu.HBM(dims, dtype)


def limit(mib):
    return pltpu.CompilerParams(vmem_limit_bytes=mib << 20)


def shape(dims, dtype):
    return jax.ShapeDtypeStruct(dims, dtype)


def body(
    tokens,
    in_gain,
    in_z,
    in_x,
    in_bc,
    in_dt,
    conv_x,
    conv_bc,
    dt_bias,
    a_log,
    d_skip,
    norm_gain,
    out_w,
    post_gain,
    sh_gate,
    sh_up,
    sh_down,
    ex_gate,
    ex_up,
    ex_down,
    routes,
    gates,
    lengths,
    cache_slot,
):
    seq_idx = lax.axis_index("seq")
    exp_idx = lax.axis_index("exp")
    where_am_i = jnp.reshape(exp_idx, (1,)).astype(jnp.int32)
    width = tokens.shape[1]
    row_count = 8 * ROWS

    up = over_exp(tokens, PLUS)
    down = over_exp(tokens, MINUS)
    mate = over_exp(tokens, MATE)

    (w_all, w_dt, bias, rate, skip, taps, seg_ext, seg_row, gain_in, gain_mix, gain_post, meta) = pl.pallas_call(
        tables_kernel,
        out_shape=(
            vmem((width, 1024), BF16),
            vmem((LANES, width), BF16),
            vmem((1, LANES), F32),
            vmem((1, LANES), F32),
            vmem((1, WIDE), F32),
            vmem((4, 640), F32),
            vmem((row_count + 16, 1), jnp.int32),
            vmem((8, CHUNK), jnp.int32),
            vmem((1, width), F32),
            vmem((1, WIDE), F32),
            vmem((1, width), F32),
            shape((80,), jnp.int32),
        ),
        in_specs=[SM] * 6 + [VM] * 6 + [ANY] * 3,
        out_specs=(VM,) * 11 + (SM,),
        scratch_shapes=[pltpu.SemaphoreType.DMA((3,))],
        compiler_params=limit(16),
        name="tables",
    )(
        seq_idx.reshape(1).astype(jnp.int32),
        *far_core(
            lengths,
            cache_slot,
            dt_bias,
            a_log,
            d_skip,
            in_dt.T,
            conv_x,
            conv_bc,
            in_gain,
            norm_gain,
            post_gain,
            in_x,
            in_bc,
            in_z,
        ),
    )

    picks = (routes[:, :, None] == jnp.arange(64, dtype=jnp.int32)).astype(F32)
    named = jnp.sum(picks, axis=1)
    weight = jnp.sum(picks * gates[:, :, None], axis=1)
    earlier = (jnp.arange(ROWS)[:, None] > jnp.arange(ROWS)[None, :]).astype(BF16)
    rank = jnp.dot(earlier, named.astype(BF16), preferred_element_type=F32)
    rank = jnp.where(named > 0, rank, -1.0)
    slots = jnp.arange(1024, dtype=jnp.int32)
    fan = (slots[None, :] // CAP == jnp.arange(64, dtype=jnp.int32)[:, None]).astype(BF16)
    rank_wide = jnp.dot(rank.astype(BF16), fan, preferred_element_type=F32)
    hit = rank_wide == (slots % CAP).astype(F32)[None, :]
    w_high = weight.astype(BF16)
    mix = jnp.where(hit, jnp.dot(w_high, fan, preferred_element_type=F32), 0.0).astype(BF16)
    spots = hit.astype(BF16).T

    def project(plan, blocks, *done):
        return pl.pallas_call(
            functools.partial(project_kernel, plan=plan),
            out_shape=(
                vmem((row_count, 640), BF16),
                vmem((row_count, LANES), F32),
                vmem((row_count, LANES), F32),
                vmem((row_count, WIDE), F32),
            ),
            in_specs=[SM] + [VM] * (len(blocks) + 5 + len(done)),
            out_specs=(VM,) * 4,
            scratch_shapes=[pltpu.VMEM((2 * ROWS, width), BF16)],
            input_output_aliases={len(blocks) + 6 + i: i for i in range(len(done))},
            compiler_params=limit(16),
            name="project",
        )(where_am_i, *near_core(*blocks, gain_in, w_all, w_dt, bias, rate, *done))

    done = project(((0, ((0, 0, ROWS, True, 0), (1, 0, ROWS, False, 0))),), (tokens, mate))
    up, down, done = lax.optimization_barrier((up, down, done))
    both, up_low, down_high = pl.pallas_call(
        join_kernel,
        out_shape=(
            vmem((2 * ROWS, width), BF16),
            vmem((HALF, width), BF16),
            vmem((HALF, width), BF16),
        ),
        in_specs=[VM] * 2,
        out_specs=(VM,) * 3,
        compiler_params=limit(16),
        name="join",
    )(*near_core(up, down))
    far_a = over_exp(up_low, PLUS)
    far_b = over_exp(down_high, MINUS)
    both_mate = over_exp(both, MATE)
    done = project(
        (
            (3, ((0, 0, ROWS, True, 0), (1, 0, ROWS, False, 0))),
            (1, ((0, ROWS, ROWS, True, 0), (1, ROWS, ROWS, False, 0))),
        ),
        (both, both_mate),
        *done,
    )
    far_a, far_b, done = lax.optimization_barrier((far_a, far_b, done))
    conv_in, step, cum, z = project(
        ((2, ((0, 0, HALF, True, 0), (1, 0, HALF, True, HALF), (2, 0, HALF, False, 0), (3, 0, HALF, False, HALF))),),
        (far_a, far_b, over_exp(far_a, MATE), over_exp(far_b, MATE)),
        *done,
    )

    edge = ahead(conv_in[row_count - 16 :], 1)
    x_rows, bc_rows, fresh = pl.pallas_call(
        conv_kernel,
        out_shape=(
            vmem((row_count, WIDE), BF16),
            vmem((row_count, 2 * STATE), BF16),
            vmem((8, STATE, WIDE), F32),
        ),
        in_specs=[SM] + [VM] * 5,
        out_specs=(VM,) * 3,
        compiler_params=limit(16),
        name="conv",
    )(meta, *near_core(conv_in, seg_ext, step, cum, taps))
    x_rows, bc_rows, states, sent, past = pl.pallas_call(
        chain_kernel,
        out_shape=(
            vmem((row_count, WIDE), BF16),
            vmem((row_count, 2 * STATE), BF16),
            vmem((8, STATE, WIDE), BF16),
            vmem((STATE + 16, WIDE), BF16),
            vmem((8, LANES), F32),
        ),
        in_specs=[SM] + [VM] * 9,
        out_specs=(VM,) * 5,
        input_output_aliases={8: 0, 9: 1},
        compiler_params=limit(16),
        name="chain",
    )(meta, *near_core(conv_in, edge, seg_ext, step, cum, taps, fresh, x_rows, bc_rows))

    def local_part(first, last, *done):
        return pl.pallas_call(
            functools.partial(local_kernel, first=first, last=last),
            out_shape=vmem((row_count, WIDE), F32),
            in_specs=[SM] + [VM] * (8 + len(done)),
            out_specs=VM,
            input_output_aliases={9: 0} if done else {},
            compiler_params=limit(16),
            name="local",
        )(meta, *near_core(x_rows, bc_rows, cum, step, seg_ext, seg_row, states, skip, *done))

    got = ahead(sent, 1)
    y_local = local_part(0, 4)
    got, y_local = lax.optimization_barrier((got, y_local))
    two = pl.pallas_call(
        pair_kernel,
        out_shape=vmem((STATE + 16, WIDE), BF16),
        in_specs=[VM, VM],
        out_specs=VM,
        compiler_params=limit(16),
        name="pair",
    )(*near_core(sent, got))
    two, y_local = lax.optimization_barrier((two, y_local))
    near = ahead(two, 1)
    far = ahead(two, 3)
    y_local = local_part(4, 8, y_local)
    near, far, y_local, states = lax.optimization_barrier((near, far, y_local, states))

    def project_out(mate, *other):
        wide = width + LANES
        if mate:
            outs = vmem((4, ROWS, wide), BF16)
        else:
            outs = tuple(vmem((rows, wide), BF16) for rows in (ROWS, ROWS, ROWS, HALF, HALF))
        return pl.pallas_call(
            functools.partial(out_kernel, mate=mate),
            out_shape=outs,
            in_specs=[SM, SM] + [VM] * (10 + len(other)),
            out_specs=VM if mate else (VM,) * 5,
            scratch_shapes=[pltpu.VMEM((4 * ROWS, WIDE), BF16)],
            compiler_params=limit(16),
            name="out_mate" if mate else "out_own",
        )(
            where_am_i,
            meta,
            *near_core(y_local, bc_rows, cum, seg_ext, past, z, near, far, gain_mix, out_w, *other),
        )

    mate_part = project_out(True)
    swapped = over_exp(mate_part, MATE)

    mate_part, states = lax.optimization_barrier((mate_part, states))
    ends_local = pl.pallas_call(
        ends_kernel,
        out_shape=hbm((16, STATE, WIDE), BF16),
        in_specs=[SM] + [VM] * 9,
        out_specs=VM,
        compiler_params=limit(16),
        name="ends",
    )(meta, *near_core(x_rows, bc_rows, cum, step, seg_ext, states, near, far, past))
    send_a, send_b, kept_0, kept_1, kept_3 = project_out(False, swapped)
    send_a, send_b, ends_local = lax.optimization_barrier((send_a, send_b, ends_local))
    p_a = over_exp(send_a, PLUS)
    p_b = over_exp(send_b, MINUS)
    ends_all = lax.all_to_all(ends_local, "seq", split_axis=0, concat_axis=0, tiled=True)
    q_a = over_exp((kept_1.astype(F32) + p_a[:HALF].astype(F32)).astype(BF16), PLUS)
    q_b = over_exp((kept_3.astype(F32) + p_b[HALF:].astype(F32)).astype(BF16), MINUS)

    residual, normed, outgoing = pl.pallas_call(
        enter_kernel,
        out_shape=(hbm((ROWS, width), F32), hbm((ROWS, width), BF16), hbm((1024, width), BF16)),
        grid=(4,),
        in_specs=[VM] * 7 + [pl.BlockSpec((256, ROWS), lambda i: (i, 0))],
        out_specs=(VM, VM, pl.BlockSpec((256, width), lambda i: (i, 0))),
        scratch_shapes=[pltpu.VMEM((ROWS, width), BF16)],
        compiler_params=limit(16),
        name="enter",
    )(*near_core(kept_0, p_a, p_b, q_a, q_b, tokens, gain_post), spots)
    received = lax.all_to_all(
        outgoing.reshape(16, 4, CAP, width), "seq", split_axis=0, concat_axis=0, tiled=True
    )
    sh_gate, sh_up, sh_down, ends_all, outgoing = lax.optimization_barrier(
        (sh_gate, sh_up, sh_down, ends_all, outgoing)
    )
    final = lax.dynamic_index_in_dim(ends_all, meta[64], 0, False).astype(F32)
    state_cache = final.T.reshape(1, HEADS, HALF, STATE)
    packed = jnp.concatenate([sh_gate.T, sh_up.T, sh_down])
    half = packed.shape[0] // 2
    g_up = over_exp(packed, PLUS)
    g_down = over_exp(packed, MINUS)
    g_mate = over_exp(packed, MATE)
    received, g_up, g_down, g_mate, state_cache = lax.optimization_barrier(
        (received, g_up, g_down, g_mate, state_cache)
    )
    answers = pl.pallas_call(
        expert_kernel,
        out_shape=hbm((16, 4, CAP, width), BF16),
        grid=(4,),
        in_specs=[
            VM,
            pl.BlockSpec((None, width, 512), lambda e: (e, 0, 0)),
            pl.BlockSpec((None, width, 512), lambda e: (e, 0, 0)),
            pl.BlockSpec((None, 512, width), lambda e: (e, 0, 0)),
        ],
        out_specs=pl.BlockSpec((16, None, CAP, width), lambda e: (0, e, 0, 0)),
        compiler_params=limit(20),
        name="experts",
    )(*near_core(received), *far_core(ex_gate, ex_up, ex_down))
    returned = lax.all_to_all(answers, "seq", split_axis=0, concat_axis=0, tiled=True)
    g_up, g_down, answers = lax.optimization_barrier((g_up, g_down, answers))
    g_far = jnp.concatenate([over_exp(g_up[:half], PLUS), over_exp(g_down[half:], MINUS)])
    groups = (packed, g_mate, g_up, over_exp(g_up, MATE), g_down, over_exp(g_down, MATE), g_far, over_exp(g_far, MATE))
    base = pl.pallas_call(
        shared_kernel,
        out_shape=hbm((ROWS, width), F32),
        in_specs=[VM] * 10,
        out_specs=VM,
        compiler_params=limit(16),
        name="shared",
    )(normed, *groups, residual)
    layer_out = pl.pallas_call(
        leave_kernel,
        out_shape=shape((ROWS, width), BF16),
        in_specs=[VM] * 3,
        out_specs=VM,
        compiler_params=limit(16),
        name="leave",
    )(*near_core(returned.reshape(1024, width), mix), *far_core(base))
    return (layer_out, state_cache)


def solution(mesh):
    placed = (
        P(("seq", "exp"), None),
        P(),
        P(None, "exp"),
        P(None, "exp"),
        P(),
        P(None, "exp"),
        P(None, "exp"),
        P(),
        P("exp"),
        P("exp"),
        P("exp"),
        P("exp"),
        P("exp", None),
        P(),
        P(None, "exp"),
        P(None, "exp"),
        P("exp", None),
        P("seq", None, None),
        P("seq", None, None),
        P("seq", None, None),
        P(("seq", "exp"), None),
        P(("seq", "exp"), None),
        P(),
        P(),
    )
    return jax.shard_map(
        body,
        mesh=mesh,
        in_specs=placed,
        out_specs=(P(("seq", "exp"), None), P("seq", "exp", None, None)),
        check_vma=False,
    )
```

```python
import functools

import jax
import jax.numpy as jnp
from jax import lax
from jax.experimental import pallas as pl
from jax.experimental.pallas import tpu as pltpu
from jax.sharding import PartitionSpec as P


EPS = 1e-05
HIGH = lax.Precision.HIGHEST
F32 = jnp.float32
BF16 = jnp.bfloat16
LANES = 128
ROWS = 128
CHUNK = 128
CAP = 16
HEADS = 6
HALF = 64
WIDE = 384
STATE = 128
DI = 3072
VM = pl.BlockSpec(memory_space=pltpu.VMEM)
SM = pl.BlockSpec(memory_space=pltpu.SMEM)
ANY = pl.BlockSpec(memory_space=pl.ANY)
PLUS = [(i, (i + 2) % 8) for i in range(8)]
MINUS = [(i, (i + 6) % 8) for i in range(8)]
MATE = [(i, i ^ 1) for i in range(8)]


def near_core(*arrays):
    return [pltpu.with_memory_space_constraint(a, pltpu.VMEM) for a in arrays]


def far_core(*arrays):
    return [pltpu.with_memory_space_constraint(a, pltpu.HBM) for a in arrays]


def silu(v):
    return v * (1.0 / (1.0 + jnp.exp(-v)))


def ahead(block, distance):
    return lax.ppermute(block, "seq", [(i, i + distance) for i in range(16 - distance)])


def over_exp(block, route):
    return lax.ppermute(block, "exp", route)


def spread(cols):
    rows = cols.shape[0]
    left = lax.broadcasted_iota(jnp.int32, (rows, LANES), 1) < HALF
    parts = []
    for pair in range(HEADS // 2):
        first = jnp.broadcast_to(cols[:, 2 * pair : 2 * pair + 1], (rows, LANES))
        second = jnp.broadcast_to(cols[:, 2 * pair + 1 : 2 * pair + 2], (rows, LANES))
        parts.append(jnp.where(left, first, second))
    return jnp.concatenate(parts, axis=1)


def chip_of(where):
    return where[0] // 2


def core_of(where):
    return lax.rem(where[0], 2)


def tables_kernel(
    seq, lengths, slots, dt_bias, a_log, d_skip, in_dt, conv_x, conv_bc, g_in, g_mix, g_post, x, bc, z,
    w_all, w_dt, bias, rate, skip, taps, seg_ext, seg_row, gain_in, gain_mix, gain_post, meta, sems,
):
    copies = []
    for i, (ref, at, cols) in enumerate(((x, 0, WIDE), (bc, WIDE, 2 * STATE), (z, WIDE + 2 * STATE, WIDE))):
        copies.append(pltpu.make_async_copy(ref, w_all.at[:, at : at + cols], sems.at[i]))
    for copy in copies:
        copy.start()
    base = seq[0] * (8 * CHUNK)
    total = jnp.int32(0)
    ends = []
    for req in range(16):
        total = total + lengths[req]
        ends.append(total)

    lane = lax.broadcasted_iota(jnp.int32, (1, LANES), 1)
    wide = lax.broadcasted_iota(jnp.int32, (1, WIDE), 1)
    bias_row = jnp.zeros((1, LANES), F32)
    rate_row = jnp.zeros((1, LANES), F32)
    skip_row = jnp.zeros((1, WIDE), F32)
    for head in range(HEADS):
        bias_row = jnp.where(lane == head, dt_bias[head], bias_row)
        rate_row = jnp.where(lane == head, a_log[head], rate_row)
        skip_row = jnp.where((wide >= head * HALF) & (wide < (head + 1) * HALF), d_skip[head], skip_row)
    bias[...] = bias_row
    rate[...] = jnp.where(lane < HEADS, jnp.exp(rate_row), 0.0)
    skip[...] = skip_row
    taps[:, :WIDE] = conv_x[...]
    taps[:, WIDE:] = conv_bc[...]
    gain_in[0, :] = g_in[...]
    gain_mix[0, :] = g_mix[...]
    gain_post[0, :] = g_post[...]
    w_dt[...] = jnp.zeros_like(w_dt)
    w_dt[:HEADS, :] = in_dt[...]

    def seg_at(positions):
        found = jnp.zeros_like(positions)
        for end in ends:
            found = found + jnp.where(positions >= end, 1, 0)
        return jnp.where(positions >= 0, found, -1)

    ext_i = lax.broadcasted_iota(jnp.int32, (8 * CHUNK + 16, 1), 0)
    seg_ext[...] = seg_at(base + ext_i - 16)
    row_i = lax.broadcasted_iota(jnp.int32, (8, CHUNK), 0)
    seg_row[...] = seg_at(base + row_i * CHUNK + lax.broadcasted_iota(jnp.int32, (8, CHUNK), 1))
    for c in range(8):
        before = seg_at(base + (c * CHUNK - 1))
        meta[c] = before
        meta[8 + c] = before
        meta[16 + c] = seg_at(base + (c * CHUNK + CHUNK - 1))
        meta[24 + c] = seg_at(base + c * CHUNK)
    source = jnp.int32(0)
    for req in range(16):
        meta[32 + req] = ends[req] - 1 - base
        meta[48 + req] = slots[req]
        source = jnp.where(slots[req] == seq[0], (ends[req] - 1) // (8 * CHUNK), source)
    meta[64] = source
    for copy in copies:
        copy.wait()


def join_kernel(up, down, both, up_low, down_high):
    both[:ROWS, :] = up[...]
    both[ROWS:, :] = down[...]
    up_low[...] = up[:HALF, :]
    down_high[...] = down[HALF:, :]


def project_kernel(where, *refs, plan):
    count = 1 + max(piece[0] for _, pieces in plan for piece in pieces)
    blocks, rest = refs[:count], refs[count:]
    gain, w_all, w_dt, bias, rate = rest[:5]
    conv_out, step_out, cum_out, z_out, normed = rest[-5:]
    chip, core = chip_of(where), core_of(where)
    rows_i = lax.broadcasted_iota(jnp.int32, (CHUNK, CHUNK), 0)
    cols_i = lax.broadcasted_iota(jnp.int32, (CHUNK, CHUNK), 1)
    lower = (rows_i >= cols_i).astype(F32)
    for offset, pieces in plan:
        for index, source, rows, own, to in pieces:
            vals = blocks[index][source : source + rows, :].astype(F32)
            meansq = jnp.mean(vals * vals, axis=-1, keepdims=True)
            place = core if own else 1 - core
            start = pl.multiple_of(place * ROWS + to, HALF)
            normed[pl.ds(start, rows), :] = (vals * lax.rsqrt(meansq + EPS) * gain[...]).astype(BF16)
        rows = normed[...]
        at = pl.multiple_of(lax.rem(chip + offset, 4) * (2 * ROWS), 2 * ROWS)
        here = pl.ds(at, 2 * ROWS)
        raw = lax.dot_general(rows, w_dt[...], (((1,), (1,)), ((), ())), preferred_element_type=F32)
        raw = raw.astype(BF16).astype(F32) + bias[...]
        step = jnp.maximum(raw, 0.0) + jnp.log1p(jnp.exp(-jnp.abs(raw)))
        step_out[here, :] = step
        decay = -step * rate[...]
        for part in (0, 1):
            piece = decay[part * CHUNK : (part + 1) * CHUNK, :]
            cum_out[pl.ds(at + part * CHUNK, CHUNK), :] = jnp.dot(
                lower, piece, precision=HIGH, preferred_element_type=F32
            )
        mixed = jnp.dot(rows, w_all[...], preferred_element_type=F32).astype(BF16)
        conv_out[here, :] = mixed[:, :640]
        z_out[here, :] = silu(mixed[:, 640:].astype(F32))


def conv_chunk(prior, here, seg, w_conv):
    joined = jnp.concatenate([prior, here], axis=0)
    total = here * w_conv[3:4, :]
    own = seg[16:, :]
    for lag in (1, 2, 3):
        kept = (pltpu.roll(seg, lag, 0)[16:, :] == own).astype(F32)
        moved = pltpu.roll(joined, lag, 0)[16:, :]
        total = total + (kept * moved) * w_conv[3 - lag : 4 - lag, :]
    return silu(total).astype(BF16)


def fresh_state(mixed, step, cum, seg, last_seg):
    last = cum[CHUNK - 1 : CHUNK, :]
    tail = jnp.where(seg == last_seg, jnp.exp(last - cum), 0.0)
    drive = mixed[:, :WIDE].astype(F32) * spread(step * tail)
    return lax.dot_general(
        mixed[:, WIDE : WIDE + STATE], drive.astype(BF16), (((0,), (0,)), ((), ())), preferred_element_type=F32
    )


def conv_kernel(meta, conv_in, seg_ext, step, cum, w_conv, x_out, bc_out, fresh_out):
    for c in range(1, 8):
        start = c * CHUNK
        rows = pl.ds(start, CHUNK)
        seg = seg_ext[pl.ds(start, CHUNK + 16), :]
        prior = conv_in[pl.ds(start - 16, 16), :].astype(F32)
        mixed = conv_chunk(prior, conv_in[rows, :].astype(F32), seg, w_conv)
        x_out[rows, :] = mixed[:, :WIDE]
        bc_out[rows, :] = mixed[:, WIDE:]
        fresh_out[c] = fresh_state(mixed, step[rows, :], cum[rows, :], seg[16:, :], meta[16 + c])


def row_spread(row):
    return spread(jnp.broadcast_to(row, (8, LANES)))[:1, :]


def chain_kernel(meta, conv_in, edge, seg_ext, step, cum, w_conv, fresh, x_in, bc_in, x_out, bc_out, state_out, send_out, past_out):
    before_dev = meta[0]
    seg = seg_ext[: CHUNK + 16, :]
    mixed = conv_chunk(edge[...].astype(F32), conv_in[:CHUNK, :].astype(F32), seg, w_conv)
    x_out[:CHUNK, :] = mixed[:, :WIDE]
    bc_out[:CHUNK, :] = mixed[:, WIDE:]
    first = fresh_state(mixed, step[:CHUNK, :], cum[:CHUNK, :], seg[16:, :], meta[16])
    held = jnp.zeros((STATE, WIDE), F32)
    past = jnp.zeros((1, LANES), F32)
    for c in range(8):
        last = cum[(c + 1) * CHUNK - 1 : (c + 1) * CHUNK, :]
        state_out[c] = held.astype(BF16)
        past_out[c : c + 1, :] = past
        persist = row_spread(jnp.where(meta[16 + c] == meta[8 + c], jnp.exp(last), 0.0))
        held = persist * held + (first if c == 0 else fresh[c])
        past = past + last
    send_out[:STATE, :] = held.astype(BF16)
    passed = jnp.where(meta[16 + 7] == before_dev, jnp.exp(past), 0.0)
    wide = spread(jnp.broadcast_to(passed, (16, LANES)))
    high = wide.astype(BF16)
    low = (wide - high.astype(F32)).astype(BF16)
    row = lax.broadcasted_iota(jnp.int32, (16, WIDE), 0)
    send_out[STATE:, :] = jnp.where(row == 0, high, low)


def factor_of(message):
    both = message[STATE:, :].astype(F32)
    return both[0:1, :] + both[1:2, :]


def pair_kernel(sent, got, out):
    own_factor, got_factor = factor_of(sent), factor_of(got)
    out[:STATE, :] = (sent[:STATE, :].astype(F32) + own_factor * got[:STATE, :].astype(F32)).astype(BF16)
    wide = jnp.broadcast_to(own_factor * got_factor, (16, WIDE))
    high = wide.astype(BF16)
    low = (wide - high.astype(F32)).astype(BF16)
    row = lax.broadcasted_iota(jnp.int32, (16, WIDE), 0)
    out[STATE:, :] = jnp.where(row == 0, high, low)


def entering_state(near, far):
    return near[:STATE, :].astype(F32) + factor_of(near) * far[:STATE, :].astype(F32)


def local_kernel(meta, x_in, bc_in, cum_in, step_in, seg_ext, seg_row, state_in, skip, *rest, first, last):
    y_out = rest[-1]
    rows_i = lax.broadcasted_iota(jnp.int32, (CHUNK, CHUNK), 0)
    cols_i = lax.broadcasted_iota(jnp.int32, (CHUNK, CHUNK), 1)
    causal = rows_i >= cols_i
    left = lax.broadcasted_iota(jnp.int32, (CHUNK, LANES), 1) < HALF

    def chunk(c):
        start = c * CHUNK
        rows = pl.ds(start, CHUNK)
        x = x_in[rows, :].astype(F32)
        b_rows, c_rows = bc_in[rows, :STATE], bc_in[rows, STATE:]
        cum = cum_in[rows, :]
        cum_t = cum.T
        seg = seg_ext[pl.ds(start + 16, CHUNK), :]
        mask = causal & (seg == seg_row[pl.ds(c, 1), :])
        scores = lax.dot_general(c_rows, b_rows, (((1,), (1,)), ((), ())), preferred_element_type=F32)
        scores = jnp.where(mask, scores, 0.0)
        drive_b = (x * spread(step_in[rows, :])).astype(BF16)
        entry = jnp.where(seg == meta[8 + c], jnp.exp(cum), 0.0)
        carried = jnp.dot(c_rows, state_in[c], preferred_element_type=F32)
        total = spread(entry) * carried + skip[...] * x
        for pair in range(HEADS // 2):
            block = drive_b[:, pair * LANES : (pair + 1) * LANES]
            zero = jnp.zeros_like(block)
            acc = total[:, pair * LANES : (pair + 1) * LANES]
            for side in (0, 1):
                head = 2 * pair + side
                gap = jnp.minimum(cum[:, head : head + 1] - cum_t[head : head + 1, :], 0.0)
                weights = (scores * jnp.exp(gap)).astype(BF16)
                value = jnp.where(left, block, zero) if side == 0 else jnp.where(left, zero, block)
                acc = acc + jnp.dot(weights, value, preferred_element_type=F32)
            y_out[rows, pair * LANES : (pair + 1) * LANES] = acc

    for c in range(first, last):
        chunk(c)


def ends_kernel(meta, x_in, bc_in, cum_in, step_in, seg_ext, state_in, near, far, past, ends_out, held, sems):
    def close(req, carry):
        at = meta[32 + req]

        @pl.when((at >= 0) & (at < 8 * CHUNK))
        def _():
            c = at // CHUNK
            rows = pl.ds(pl.multiple_of(c * CHUNK, CHUNK), CHUNK)
            cum = cum_in[rows, :]
            cum_end = cum_in[pl.ds(at, 1), :]
            seg = seg_ext[pl.ds(c * CHUNK + 16, CHUNK), :]
            weight = jnp.where(seg == req, jnp.exp(jnp.minimum(cum_end - cum, 0.0)), 0.0)
            drive = x_in[rows, :].astype(F32) * spread(step_in[rows, :] * weight)
            fresh = lax.dot_general(
                bc_in[rows, :STATE], drive.astype(BF16), (((0,), (0,)), ((), ())), preferred_element_type=F32
            )
            hold = row_spread(jnp.where(req == meta[8 + c], jnp.exp(cum_end), 0.0))
            since = cum_end + past[pl.ds(c, 1), :]
            opened = row_spread(jnp.where(req == meta[0], jnp.exp(since), 0.0))
            value = fresh + hold * state_in[c].astype(F32) + opened * entering_state(near, far)
            slot = meta[48 + req]
            held[slot] = value.astype(BF16)
            pltpu.make_async_copy(held.at[slot], ends_out.at[slot], sems.at[slot]).start()

        return carry

    def finish(req, carry):
        at = meta[32 + req]

        @pl.when((at >= 0) & (at < 8 * CHUNK))
        def _():
            slot = meta[48 + req]
            pltpu.make_async_copy(held.at[slot], ends_out.at[slot], sems.at[slot]).wait()

        return carry

    lax.fori_loop(meta[24], meta[16 + 7] + 1, close, 0)
    lax.fori_loop(meta[24], meta[16 + 7] + 1, finish, 0)


def out_kernel(where, meta, y_in, bc_in, cum_in, seg_ext, past, z_in, near, far, norm_gain, w_out, *rest, mate):
    gated = rest[-1]
    core = core_of(where)
    if mate:
        core = 1 - core
    state = entering_state(near, far).astype(BF16)
    squares = []
    for rel in range(4):
        block = lax.rem(chip_of(where) + rel, 4) * 2 + core
        start = pl.multiple_of(block * ROWS, ROWS)
        rows = pl.ds(start, ROWS)
        carried = jnp.dot(bc_in[rows, STATE:], state, preferred_element_type=F32)
        seg = seg_ext[pl.ds(start + 16, ROWS), :]
        lead = jnp.where(seg == meta[0], jnp.exp(cum_in[rows, :] + past[pl.ds(block, 1), :]), 0.0)
        g = (y_in[rows, :] + spread(lead) * carried) * z_in[rows, :]
        squares.append(jnp.broadcast_to(jnp.sum(g * g, axis=1, keepdims=True), (ROWS, LANES)))
        gated[rel * ROWS : (rel + 1) * ROWS, :] = (g * norm_gain[...]).astype(BF16)

    if mate:
        (out,) = rest[:-1]
        for pair in (0, 1):
            mixed = jnp.dot(gated[pair * 256 : (pair + 1) * 256, :], w_out[...], preferred_element_type=F32)
            for rel in (2 * pair, 2 * pair + 1):
                at = (rel - 2 * pair) * ROWS
                out[rel, :, :1536] = mixed[at : at + ROWS, :].astype(BF16)
                out[rel, :, 1536:] = squares[rel].astype(BF16)
    else:
        other, send_a, send_b, kept_0, kept_1, kept_3 = rest[:-1]
        places = (
            ((kept_0, 0), (kept_0, HALF)),
            ((kept_1, 0), (send_a, HALF)),
            ((send_a, 0), (send_b, HALF)),
            ((send_b, 0), (kept_3, 0)),
        )
        for pair in (0, 1):
            mixed = jnp.dot(gated[pair * 256 : (pair + 1) * 256, :], w_out[...], preferred_element_type=F32)
            for rel in (2 * pair, 2 * pair + 1):
                at = (rel - 2 * pair) * ROWS
                for side, (ref, to) in enumerate(places[rel]):
                    lo = side * HALF
                    ref[to : to + HALF, :1536] = (
                        mixed[at + lo : at + lo + HALF, :] + other[rel, lo : lo + HALF, :1536].astype(F32)
                    ).astype(BF16)
                    ref[to : to + HALF, 1536:] = (
                        squares[rel][lo : lo + HALF, :] + other[rel, lo : lo + HALF, 1536:].astype(F32)
                    ).astype(BF16)


def enter_kernel(h0, p_a, p_b, q_a, q_b, tokens, gain, spots, residual_out, normed_out, outgoing, held, kept, sems):
    @pl.when(pl.program_id(0) == 0)
    def _():
        first = h0[:HALF, :].astype(F32) + p_b[:HALF, :].astype(F32) + q_a[...].astype(F32)
        second = h0[HALF:, :].astype(F32) + p_a[HALF:, :].astype(F32) + q_b[...].astype(F32)
        both = jnp.concatenate([first, second], axis=0)
        scale = lax.rsqrt(both[:, 1536:1537] * (1.0 / DI) + EPS)
        residual = tokens[...].astype(F32) + both[:, :1536] * scale
        kept[...] = residual
        pltpu.make_async_copy(kept, residual_out, sems.at[0]).start()
        meansq = jnp.mean(residual * residual, axis=-1, keepdims=True)
        held[...] = (residual * lax.rsqrt(meansq + EPS) * gain[...]).astype(BF16)
        pltpu.make_async_copy(held, normed_out, sems.at[1]).start()

    outgoing[...] = jnp.dot(spots[...], held[...], preferred_element_type=F32).astype(BF16)

    @pl.when(pl.program_id(0) == pl.num_programs(0) - 1)
    def _():
        pltpu.make_async_copy(kept, residual_out, sems.at[0]).wait()
        pltpu.make_async_copy(held, normed_out, sems.at[1]).wait()


def expert_kernel(rows_ref, gate, up, down, out, gates, ups, downs, sems):
    expert = pl.program_id(0)

    def copies(e):
        return [
            pltpu.make_async_copy(src.at[e], dst.at[e], sems.at[i, e])
            for i, (src, dst) in enumerate(((gate, gates), (up, ups), (down, downs)))
        ]

    @pl.when(expert == 0)
    def _():
        for e in (0, 1):
            for copy in copies(e):
                copy.start()

    @pl.when(expert < 2)
    def _():
        for copy in copies(expert + 2):
            copy.start()

    gate_copy, up_copy, down_copy = copies(expert)
    rows = rows_ref[:, expert].reshape(256, 1536)
    gate_copy.wait()
    g = jnp.dot(rows, gates[expert], preferred_element_type=F32)
    up_copy.wait()
    u = jnp.dot(rows, ups[expert], preferred_element_type=F32)
    hidden = (silu(g) * u).astype(BF16)
    down_copy.wait()
    out[...] = jnp.dot(hidden, downs[expert], preferred_element_type=F32).astype(BF16).reshape(16, CAP, 1536)


def shared_kernel(rows_ref, w0, w1, w2, w3, w4, w5, w6, w7, residual, out):
    rows = rows_ref[...]
    total = residual[...]
    for w in (w0, w1, w2, w3, w4, w5, w6, w7):
        both = lax.dot_general(rows, w[:256, :], (((1,), (1,)), ((), ())), preferred_element_type=F32)
        hidden = (silu(both[:, :128]) * both[:, 128:]).astype(BF16)
        total = total + jnp.dot(hidden, w[256:, :], preferred_element_type=F32)
    out[...] = total


def leave_kernel(returned, mix, base, out, held, sems):
    copy = pltpu.make_async_copy(base, held, sems.at[0])
    copy.start()
    routed = jnp.dot(mix[...], returned[...], preferred_element_type=F32)
    copy.wait()
    out[...] = (held[...] + routed).astype(BF16)


def vmem(dims, dtype):
    return pltpu.VMEM(dims, dtype)


def hbm(dims, dtype):
    return pltpu.HBM(dims, dtype)


def limit(mib):
    return pltpu.CompilerParams(vmem_limit_bytes=mib << 20)


def shape(dims, dtype):
    return jax.ShapeDtypeStruct(dims, dtype)


def body(
    tokens,
    in_gain,
    in_z,
    in_x,
    in_bc,
    in_dt,
    conv_x,
    conv_bc,
    dt_bias,
    a_log,
    d_skip,
    norm_gain,
    out_w,
    post_gain,
    sh_gate,
    sh_up,
    sh_down,
    ex_gate,
    ex_up,
    ex_down,
    routes,
    gates,
    lengths,
    cache_slot,
):
    seq_idx = lax.axis_index("seq")
    exp_idx = lax.axis_index("exp")
    where_am_i = jnp.reshape(exp_idx, (1,)).astype(jnp.int32)
    width = tokens.shape[1]
    row_count = 8 * ROWS

    up = over_exp(tokens, PLUS)
    down = over_exp(tokens, MINUS)
    mate = over_exp(tokens, MATE)

    (w_all, w_dt, bias, rate, skip, taps, seg_ext, seg_row, gain_in, gain_mix, gain_post, meta) = pl.pallas_call(
        tables_kernel,
        out_shape=(
            vmem((width, 1024), BF16),
            vmem((LANES, width), BF16),
            vmem((1, LANES), F32),
            vmem((1, LANES), F32),
            vmem((1, WIDE), F32),
            vmem((4, 640), F32),
            vmem((row_count + 16, 1), jnp.int32),
            vmem((8, CHUNK), jnp.int32),
            vmem((1, width), F32),
            vmem((1, WIDE), F32),
            vmem((1, width), F32),
            shape((80,), jnp.int32),
        ),
        in_specs=[SM] * 6 + [VM] * 6 + [ANY] * 3,
        out_specs=(VM,) * 11 + (SM,),
        scratch_shapes=[pltpu.SemaphoreType.DMA((3,))],
        compiler_params=limit(16),
        name="tables",
    )(
        seq_idx.reshape(1).astype(jnp.int32),
        *far_core(
            lengths,
            cache_slot,
            dt_bias,
            a_log,
            d_skip,
            in_dt.T,
            conv_x,
            conv_bc,
            in_gain,
            norm_gain,
            post_gain,
            in_x,
            in_bc,
            in_z,
        ),
    )

    def project(plan, blocks, *done):
        return pl.pallas_call(
            functools.partial(project_kernel, plan=plan),
            out_shape=(
                vmem((row_count, 640), BF16),
                vmem((row_count, LANES), F32),
                vmem((row_count, LANES), F32),
                vmem((row_count, WIDE), F32),
            ),
            in_specs=[SM] + [VM] * (len(blocks) + 5 + len(done)),
            out_specs=(VM,) * 4,
            scratch_shapes=[pltpu.VMEM((2 * ROWS, width), BF16)],
            input_output_aliases={len(blocks) + 6 + i: i for i in range(len(done))},
            compiler_params=limit(16),
            name="project",
        )(where_am_i, *near_core(*blocks, gain_in, w_all, w_dt, bias, rate, *done))

    done = project(((0, ((0, 0, ROWS, True, 0), (1, 0, ROWS, False, 0))),), (tokens, mate))
    up, down, done = lax.optimization_barrier((up, down, done))
    both, up_low, down_high = pl.pallas_call(
        join_kernel,
        out_shape=(
            vmem((2 * ROWS, width), BF16),
            vmem((HALF, width), BF16),
            vmem((HALF, width), BF16),
        ),
        in_specs=[VM] * 2,
        out_specs=(VM,) * 3,
        compiler_params=limit(16),
        name="join",
    )(*near_core(up, down))
    far_a = over_exp(up_low, PLUS)
    far_b = over_exp(down_high, MINUS)
    both_mate = over_exp(both, MATE)
    done = project(
        (
            (3, ((0, 0, ROWS, True, 0), (1, 0, ROWS, False, 0))),
            (1, ((0, ROWS, ROWS, True, 0), (1, ROWS, ROWS, False, 0))),
        ),
        (both, both_mate),
        *done,
    )
    far_a, far_b, done = lax.optimization_barrier((far_a, far_b, done))
    conv_in, step, cum, z = project(
        ((2, ((0, 0, HALF, True, 0), (1, 0, HALF, True, HALF), (2, 0, HALF, False, 0), (3, 0, HALF, False, HALF))),),
        (far_a, far_b, over_exp(far_a, MATE), over_exp(far_b, MATE)),
        *done,
    )

    edge = ahead(conv_in[row_count - 16 :], 1)
    x_rows, bc_rows, fresh = pl.pallas_call(
        conv_kernel,
        out_shape=(
            vmem((row_count, WIDE), BF16),
            vmem((row_count, 2 * STATE), BF16),
            vmem((8, STATE, WIDE), F32),
        ),
        in_specs=[SM] + [VM] * 5,
        out_specs=(VM,) * 3,
        compiler_params=limit(16),
        name="conv",
    )(meta, *near_core(conv_in, seg_ext, step, cum, taps))
    x_rows, bc_rows, states, sent, past = pl.pallas_call(
        chain_kernel,
        out_shape=(
            vmem((row_count, WIDE), BF16),
            vmem((row_count, 2 * STATE), BF16),
            vmem((8, STATE, WIDE), BF16),
            vmem((STATE + 16, WIDE), BF16),
            vmem((8, LANES), F32),
        ),
        in_specs=[SM] + [VM] * 9,
        out_specs=(VM,) * 5,
        input_output_aliases={8: 0, 9: 1},
        compiler_params=limit(16),
        name="chain",
    )(meta, *near_core(conv_in, edge, seg_ext, step, cum, taps, fresh, x_rows, bc_rows))

    def local_part(first, last, *done):
        return pl.pallas_call(
            functools.partial(local_kernel, first=first, last=last),
            out_shape=vmem((row_count, WIDE), F32),
            in_specs=[SM] + [VM] * (8 + len(done)),
            out_specs=VM,
            input_output_aliases={9: 0} if done else {},
            compiler_params=limit(16),
            name="local",
        )(meta, *near_core(x_rows, bc_rows, cum, step, seg_ext, seg_row, states, skip, *done))

    got = ahead(sent, 1)
    y_local = local_part(0, 5)
    got, y_local = lax.optimization_barrier((got, y_local))
    two = pl.pallas_call(
        pair_kernel,
        out_shape=vmem((STATE + 16, WIDE), BF16),
        in_specs=[VM, VM],
        out_specs=VM,
        compiler_params=limit(16),
        name="pair",
    )(*near_core(sent, got))
    two, y_local = lax.optimization_barrier((two, y_local))
    near = ahead(two, 1)
    far = ahead(two, 3)
    y_local = local_part(5, 8, y_local)
    near, far, y_local, states = lax.optimization_barrier((near, far, y_local, states))

    def project_out(mate, *other):
        wide = width + LANES
        if mate:
            outs = vmem((4, ROWS, wide), BF16)
        else:
            outs = tuple(vmem((rows, wide), BF16) for rows in (ROWS, ROWS, ROWS, HALF, HALF))
        return pl.pallas_call(
            functools.partial(out_kernel, mate=mate),
            out_shape=outs,
            in_specs=[SM, SM] + [VM] * (10 + len(other)),
            out_specs=VM if mate else (VM,) * 5,
            scratch_shapes=[pltpu.VMEM((4 * ROWS, WIDE), BF16)],
            compiler_params=limit(16),
            name="out_mate" if mate else "out_own",
        )(
            where_am_i,
            meta,
            *near_core(y_local, bc_rows, cum, seg_ext, past, z, near, far, gain_mix, out_w, *other),
        )

    mate_part = project_out(True)
    swapped = over_exp(mate_part, MATE)

    mate_part, states = lax.optimization_barrier((mate_part, states))
    ends_local = pl.pallas_call(
        ends_kernel,
        out_shape=hbm((16, STATE, WIDE), BF16),
        in_specs=[SM] + [VM] * 9,
        out_specs=ANY,
        scratch_shapes=[pltpu.VMEM((16, STATE, WIDE), BF16), pltpu.SemaphoreType.DMA((16,))],
        compiler_params=limit(16),
        name="ends",
    )(meta, *near_core(x_rows, bc_rows, cum, step, seg_ext, states, near, far, past))
    send_a, send_b, kept_0, kept_1, kept_3 = project_out(False, swapped)
    send_a, send_b, ends_local = lax.optimization_barrier((send_a, send_b, ends_local))
    routes, gates, send_a, send_b = lax.optimization_barrier((routes, gates, send_a, send_b))
    picks = (routes[:, :, None] == jnp.arange(64, dtype=jnp.int32)).astype(F32)
    named = jnp.sum(picks, axis=1)
    weight = jnp.sum(picks * gates[:, :, None], axis=1)
    earlier = (jnp.arange(ROWS)[:, None] > jnp.arange(ROWS)[None, :]).astype(BF16)
    rank = jnp.dot(earlier, named.astype(BF16), preferred_element_type=F32)
    rank = jnp.where(named > 0, rank, -1.0)
    slots = jnp.arange(1024, dtype=jnp.int32)
    fan = (slots[None, :] // CAP == jnp.arange(64, dtype=jnp.int32)[:, None]).astype(BF16)
    rank_wide = jnp.dot(rank.astype(BF16), fan, preferred_element_type=F32)
    hit = rank_wide == (slots % CAP).astype(F32)[None, :]
    w_high = weight.astype(BF16)
    mix = jnp.where(hit, jnp.dot(w_high, fan, preferred_element_type=F32), 0.0).astype(BF16)
    spots = hit.astype(BF16).T

    p_a = over_exp(send_a, PLUS)
    p_b = over_exp(send_b, MINUS)
    ends_all = lax.all_to_all(ends_local, "seq", split_axis=0, concat_axis=0, tiled=True)
    q_a = over_exp((kept_1.astype(F32) + p_a[:HALF].astype(F32)).astype(BF16), PLUS)
    q_b = over_exp((kept_3.astype(F32) + p_b[HALF:].astype(F32)).astype(BF16), MINUS)

    residual, normed, outgoing = pl.pallas_call(
        enter_kernel,
        out_shape=(hbm((ROWS, width), F32), hbm((ROWS, width), BF16), hbm((1024, width), BF16)),
        grid=(4,),
        in_specs=[VM] * 7 + [pl.BlockSpec((256, ROWS), lambda i: (i, 0))],
        out_specs=(ANY, ANY, pl.BlockSpec((256, width), lambda i: (i, 0))),
        scratch_shapes=[
            pltpu.VMEM((ROWS, width), BF16),
            pltpu.VMEM((ROWS, width), F32),
            pltpu.SemaphoreType.DMA((2,)),
        ],
        compiler_params=limit(16),
        name="enter",
    )(*near_core(kept_0, p_a, p_b, q_a, q_b, tokens, gain_post), spots)
    received = lax.all_to_all(
        outgoing.reshape(16, 4, CAP, width), "seq", split_axis=0, concat_axis=0, tiled=True
    )
    sh_gate, sh_up, sh_down, ends_all, outgoing = lax.optimization_barrier(
        (sh_gate, sh_up, sh_down, ends_all, outgoing)
    )
    final = lax.dynamic_index_in_dim(ends_all, meta[64], 0, False).astype(F32)
    state_cache = final.T.reshape(1, HEADS, HALF, STATE)
    packed = jnp.concatenate([sh_gate.T, sh_up.T, sh_down])
    half = packed.shape[0] // 2
    g_up = over_exp(packed, PLUS)
    g_down = over_exp(packed, MINUS)
    g_mate = over_exp(packed, MATE)
    received, g_up, g_down, g_mate, state_cache = lax.optimization_barrier(
        (received, g_up, g_down, g_mate, state_cache)
    )
    answers = pl.pallas_call(
        expert_kernel,
        out_shape=hbm((16, 4, CAP, width), BF16),
        grid=(4,),
        in_specs=[VM, ANY, ANY, ANY],
        out_specs=pl.BlockSpec((16, None, CAP, width), lambda e: (0, e, 0, 0)),
        scratch_shapes=[
            pltpu.VMEM((4, width, 512), BF16),
            pltpu.VMEM((4, width, 512), BF16),
            pltpu.VMEM((4, 512, width), BF16),
            pltpu.SemaphoreType.DMA((3, 4)),
        ],
        compiler_params=limit(32),
        name="experts",
    )(*near_core(received), *far_core(ex_gate, ex_up, ex_down))
    returned = lax.all_to_all(answers, "seq", split_axis=0, concat_axis=0, tiled=True)
    g_up, g_down, answers = lax.optimization_barrier((g_up, g_down, answers))
    g_far = jnp.concatenate([over_exp(g_up[:half], PLUS), over_exp(g_down[half:], MINUS)])
    groups = (packed, g_mate, g_up, over_exp(g_up, MATE), g_down, over_exp(g_down, MATE), g_far, over_exp(g_far, MATE))
    base = pl.pallas_call(
        shared_kernel,
        out_shape=hbm((ROWS, width), F32),
        in_specs=[VM] * 10,
        out_specs=VM,
        compiler_params=limit(16),
        name="shared",
    )(normed, *groups, residual)
    layer_out = pl.pallas_call(
        leave_kernel,
        out_shape=shape((ROWS, width), BF16),
        in_specs=[VM, VM, ANY],
        out_specs=VM,
        scratch_shapes=[pltpu.VMEM((ROWS, width), F32), pltpu.SemaphoreType.DMA((1,))],
        compiler_params=limit(16),
        name="leave",
    )(*near_core(returned.reshape(1024, width), mix), *far_core(base))
    return (layer_out, state_cache)


def solution(mesh):
    placed = (
        P(("seq", "exp"), None),
        P(),
        P(None, "exp"),
        P(None, "exp"),
        P(),
        P(None, "exp"),
        P(None, "exp"),
        P(),
        P("exp"),
        P("exp"),
        P("exp"),
        P("exp"),
        P("exp", None),
        P(),
        P(None, "exp"),
        P(None, "exp"),
        P("exp", None),
        P("seq", None, None),
        P("seq", None, None),
        P("seq", None, None),
        P(("seq", "exp"), None),
        P(("seq", "exp"), None),
        P(),
        P(),
    )
    return jax.shard_map(
        body,
        mesh=mesh,
        in_specs=placed,
        out_specs=(P(("seq", "exp"), None), P("seq", "exp", None, None)),
        check_vma=False,
    )
```
